32 devices in a mesh: chan: 8 (over z, x), src: 4 (over y, core).
Axes of the slice: x: 2, y: 2, z: 4, core: 2. Of those that a mesh axis runs over, the one named last changes fastest.
Arguments:
- records: bfloat16 [1024, 4096], P('chan'), may hold values from -600 to 600
- virtual_sources: int32 [64], P('src'), may hold values from 0 to 1023
- pair_group: int32 [4096, 1], P(('chan', 'src')), may hold values from 0 to 7; in each aligned block of 128 rows (0 to 127, 128 to 255, ...) at most 32 rows name the same one
- pair_receiver: int32 [4096], P(('chan', 'src')), may hold values from 0 to 127
- pair_source: int32 [4096], P(('chan', 'src')), may hold values from 0 to 15
- observed: float32 [4096, 2048], P(('chan', 'src')), may hold values from -6 to 6
Outputs:
- adjoint_source: float32 [1024, 4096], P(('chan', 'src'))
- pair_misfit: float32 [4096], P(('chan', 'src'))
The draws below stay inside these ranges and needn't reach their ends.
Inputs may be any that keep to these rules, and one draw needn't show every extreme that they name: `pair_group`: among the 128 pairs listed by one device at most 32 name the same channel group, and in every draw some device lists exactly 32 pairs for some group.
All inputs are finite; a program needn't handle non-finite values.
Results may differ from the reference program's by a relative error of at most 0.0021.
Values sent between devices are 32-bit elements; how exact they have to be, the bound alone decides.
No kernel may reach another device: no remote copies, remote signals or barrier semaphores. Data moves between devices by JAX's collectives and lax.ppermute only.
A program may use at most 64 MiB of HBM per device.

```python
import math
import jax
import jax.numpy as jnp
import numpy as np
from jax import lax

NT = 4096
NF = 1024
K0 = 64
CH_DEV = 128
SRC_DEV = 16
PAIR_DEV = 128
CHANNELS = 1024
NSRC = 64
PAIRS = 4096
CAP = 32
N_CHAN = 8
N_SRC = 4


def draw_records(key, part):
    key_base, key_rows, key_times = jax.random.split(key, 3)
    base_values = jnp.clip(jax.random.normal(key_base, (CHANNELS, NT), jnp.float32), -6.0, 6.0)
    row_scale = jnp.exp(jax.random.uniform(key_rows, (CHANNELS, 1), jnp.float32, 0.0, math.log(10.0)))
    time_scale = jnp.exp(jax.random.uniform(key_times, (1, NT), jnp.float32, 0.0, math.log(10.0)))
    return jnp.clip(base_values * row_scale * time_scale, -600.0, 600.0).astype(jnp.bfloat16)


def set_ends(drawn, key, smallest, largest):
    extent = drawn.shape
    place = [jax.random.randint(jax.random.fold_in(key, axis), (), 0, extent[axis]) for axis in range(len(extent))]
    drawn = drawn.at[tuple(place)].set(smallest)
    longest = extent.index(max(extent))
    place[longest] = (place[longest] + 1) % extent[longest]
    return drawn.at[tuple(place)].set(largest)


def levels(rng, dims, cuts, smallest, top_value):
    gain, own = 1.0, jax.random.fold_in(rng, 6)
    for position, blocks in cuts:
        heights = jnp.exp(jax.random.uniform(jax.random.fold_in(own, position), (blocks,), jnp.float32, smallest / len(cuts), top_value / len(cuts)))
        gain = gain * jnp.repeat(heights, dims[position] // blocks).reshape([-1 if axis == position else 1 for axis in range(len(dims))])
    return gain


def routed_block(rng, own, number, rows, amount, top, reach, slope):
    order = jax.random.permutation(rng, amount)
    crowded, common = portions_of(amount, rows * top, reach, slope, True), portions_of(amount, rows * top, reach, slope, False)
    places = jnp.arange(amount)

    def named(sizes, turn):
        used = int((sizes > 0).sum())
        fixed = max(1, used // 4)
        passed = fixed + (places - fixed + turn * (used - fixed)) % max(1, amount - fixed)
        return jnp.zeros((amount,), jnp.int32).at[order[jnp.where(places < fixed, places, passed)]].set(jnp.asarray(sizes, jnp.int32))

    sizes = jnp.where(number % 4 == 0, named(crowded, number // 4), named(common, number - number // 4 - 1))
    mixed = jax.random.permutation(jax.random.fold_in(own, 3), amount)
    giver, receiver = mixed[0:amount // 2 * 2:2], mixed[1:amount // 2 * 2:2]
    margin = jnp.minimum(sizes[giver] - 1, reach - sizes[receiver]) // 2
    margin = jnp.where((giver == order[0]) | (receiver == order[0]) | (sizes[receiver] == 0), 0, jnp.maximum(margin, 0))
    passed = jax.random.randint(jax.random.fold_in(own, 4), (amount // 2,), 0, 1 << 20) % (margin + 1)
    sizes = sizes.at[giver].add(-passed).at[receiver].add(passed)
    items = jnp.searchsorted(jnp.cumsum(sizes), jnp.arange(rows * top), side="right").astype(jnp.int32)
    table = items.reshape(top, rows).T
    table = table[jax.random.permutation(jax.random.fold_in(own, 1), rows)]
    turn = jax.random.randint(jax.random.fold_in(own, 2), (rows, 1), 0, top)
    return jnp.take_along_axis(table, (jnp.arange(top)[None, :] + turn) % top, axis=1)


def portions_of(count, total, bound, lean, full):
    loads = [(1 << 20) // math.isqrt(grade ** lean) + 1 for grade in range(1, count + 1)]
    largest = bound if full else min(bound, max(-(-total // count), total * loads[0] // sum(loads)))
    least = 1 if total - largest >= count - 1 else 0
    counts, rest = [largest] + [least] * (count - 1), total - largest - least * (count - 1)
    while rest > 0:
        movable = [i for i in range(1, count) if counts[i] < largest] or [i for i in range(1, count) if counts[i] < bound]
        mass, left = sum([loads[i] for i in movable]), rest
        for i in movable:
            more = min(bound - counts[i], max(1, left * loads[i] // mass), rest)
            counts[i] = counts[i] + more
            rest = rest - more
    return np.array(counts)


def scatter_about(own_key, dims, deviation, bound, shards=(), held_as=jnp.bfloat16):
    entries = deviation * jax.random.normal(own_key, dims, jnp.float32)
    if shards:
        entries = entries * levels(own_key, dims, shards, -0.22, 0.18)
    return jnp.clip(entries, -bound, bound).astype(held_as)


def setup_inputs(seed: int = 0) -> dict:
    key_of = jax.random.split(jax.random.key(seed), 7)
    records = draw_records(jax.random.fold_in(key_of[6], 71), 0)
    virtual_sources = set_ends(jax.random.randint(key_of[1], (NSRC,), 0, CHANNELS), jax.random.fold_in(key_of[1], 1), 0, CHANNELS - 1).astype(jnp.int32)
    pair_group_keys = jax.random.split(jax.random.fold_in(key_of[2], 1), PAIRS // PAIR_DEV)
    pair_group_turns = jax.random.permutation(jax.random.fold_in(key_of[2], 3), PAIRS // PAIR_DEV)
    pair_group = jax.vmap(lambda own, number: routed_block(jax.random.fold_in(key_of[2], 2), own, number, PAIR_DEV, N_CHAN, 1, CAP, 2))(pair_group_keys, pair_group_turns).reshape((PAIRS, 1))
    pair_receiver = set_ends(jax.random.randint(key_of[3], (PAIRS,), 0, CH_DEV), jax.random.fold_in(key_of[3], 1), 0, CH_DEV - 1).astype(jnp.int32)
    pair_source = set_ends(jax.random.randint(key_of[4], (PAIRS,), 0, SRC_DEV), jax.random.fold_in(key_of[4], 1), 0, SRC_DEV - 1).astype(jnp.int32)
    observed = scatter_about(key_of[5], (PAIRS, 2 * NF), 1.0, 6.0, ((0, 32),), jnp.float32)
    return dict(records=records, virtual_sources=virtual_sources, pair_group=pair_group, pair_receiver=pair_receiver, pair_source=pair_source, observed=observed)


def fourier_basis(offset, length):
    sample_times = offset + jnp.arange(length, dtype=jnp.int32)[:, None]
    band_bins = K0 + jnp.arange(NF, dtype=jnp.int32)[None, :]
    phase_index = band_bins * sample_times % (2 * NT)
    angles = phase_index.astype(jnp.float32) * (math.pi / NT)
    return jnp.concatenate([jnp.cos(angles), -jnp.sin(angles)], axis=1)

def whiten(spectra):
    band_power = lax.optimization_barrier(jnp.sum(spectra * spectra, axis=1, keepdims=True)) / NF
    return spectra / jnp.sqrt(band_power + 1e-06)

def band_taper(bin_count):
    band_bins = jnp.arange(bin_count, dtype=jnp.int32).astype(jnp.float32)
    return 0.5 - 0.5 * jnp.cos((band_bins + 0.5) * (2.0 * math.pi / bin_count))

def pair_terms(source_rows, receiver_rows, observed_rows):
    bin_count = observed_rows.shape[-1] // 2
    weights = band_taper(bin_count)
    source_real = source_rows[..., :bin_count]
    source_imag = source_rows[..., bin_count:]
    receiver_real = receiver_rows[..., :bin_count]
    receiver_imag = receiver_rows[..., bin_count:]
    corr_real = source_real * receiver_real + source_imag * receiver_imag
    corr_imag = source_real * receiver_imag - source_imag * receiver_real
    diff_real = corr_real - observed_rows[..., :bin_count]
    diff_imag = corr_imag - observed_rows[..., bin_count:]
    misfit = lax.optimization_barrier(jnp.sum(weights * (diff_real * diff_real + diff_imag * diff_imag), axis=-1)) / (2 * bin_count)
    resid_real = weights * diff_real
    resid_imag = weights * diff_imag
    term_real = resid_real * source_real - resid_imag * source_imag
    term_imag = resid_real * source_imag + resid_imag * source_real
    return (misfit, jnp.concatenate([term_real, term_imag], axis=-1))

def reference(records, virtual_sources, pair_group, pair_receiver, pair_source, observed):
    fourier_table = fourier_basis(0, NT)
    spectra = jnp.dot(records, fourier_table.astype(jnp.bfloat16), preferred_element_type=jnp.float32)
    whitened = whiten(spectra)
    sources = jnp.take(whitened, virtual_sources, axis=0)
    listing = jnp.arange(PAIRS, dtype=jnp.int32)
    source_index = listing // PAIR_DEV % N_SRC * SRC_DEV + pair_source
    receiver_index = pair_group[:, 0] * CH_DEV + pair_receiver

    def one_block(adjoint, block_index):
        offset = (block_index * PAIR_DEV).astype(jnp.int32)
        source_block = lax.dynamic_slice_in_dim(source_index, offset, PAIR_DEV)
        receiver_block = lax.dynamic_slice_in_dim(receiver_index, offset, PAIR_DEV)
        observed_block = lax.dynamic_slice_in_dim(observed, offset, PAIR_DEV, 0)
        misfit, adjoint_term = pair_terms(jnp.take(sources, source_block, axis=0), jnp.take(whitened, receiver_block, axis=0), observed_block)
        return (adjoint.at[receiver_block].add(adjoint_term), misfit)
    adjoint_spectra, misfits = lax.scan(one_block, jnp.zeros((CHANNELS, 2 * NF), jnp.float32), jnp.arange(PAIRS // PAIR_DEV, dtype=jnp.int32))
    adjoint_source = jnp.dot(adjoint_spectra, fourier_table.T, precision=lax.Precision.HIGHEST, preferred_element_type=jnp.float32) * (1.0 / math.sqrt(NF))
    return (adjoint_source, misfits.reshape(PAIRS))
```

```python
import functools
import math

import jax
import jax.numpy as jnp
import numpy as np
from jax import lax
from jax.experimental import pallas as pl
from jax.experimental.pallas import tpu as pltpu
from jax.sharding import PartitionSpec as P


K0 = 64
LANES = 128
CUT = 5
FIRST = (6, 7, 2, 3, 1)
MIDDLE = 4
LAST = 5
BASE = 64
F32 = jnp.float32
BF16 = jnp.bfloat16
VMEM = pl.BlockSpec(memory_space=pltpu.VMEM)
NT_DIMS = (((1,), (1,)), ((), ()))


def mm(a, b):
    return jnp.dot(a, b, preferred_element_type=F32)


def split2(x):
    hi = x.astype(BF16)
    return hi, (x - hi.astype(F32)).astype(BF16)


def split3(x):
    hi = x.astype(BF16)
    rest = x - hi.astype(F32)
    mid = rest.astype(BF16)
    return hi, mid, (rest - mid.astype(F32)).astype(BF16)


def phases(products, period):
    angles = (products % period) * (2.0 * math.pi / period)
    return np.cos(angles), np.sin(angles)


def pack_kernel(parts, groups, tag_ref, group_ref, receiver_ref, source_ref, observed_ref, *outs):
    pairs = observed_ref.shape[0]
    bins = observed_ref.shape[1] // 2
    capacity = 2 * pairs // groups
    group_row = group_ref[...]
    hits = (
        lax.broadcasted_iota(jnp.int32, (max(groups, 8), pairs), 0) == group_row
    ).astype(F32)
    earlier = (
        lax.broadcasted_iota(jnp.int32, (pairs, pairs), 0)
        < lax.broadcasted_iota(jnp.int32, (pairs, pairs), 1)
    ).astype(F32)
    counts = mm(hits.astype(BF16), earlier.astype(BF16))
    rank = jnp.sum(hits * counts, axis=0, keepdims=True).astype(jnp.int32)

    def chosen(slot_row, start, stop):
        index = start + lax.broadcasted_iota(jnp.int32, (stop - start, pairs), 0)
        return (index == slot_row).astype(F32).astype(BF16)

    if len(outs) > len(parts):
        code_ref, slot_ref = outs[-2:]
        slot_row = group_row * capacity + rank
        slot_ref[...] = slot_row
        labels = jnp.concatenate(
            [receiver_ref[...] + 1, source_ref[...]] + [jnp.zeros((6, pairs), jnp.int32)], axis=0
        ).astype(F32).astype(BF16)
        sent = lax.dot_general(
            labels, chosen(slot_row, 0, groups * capacity), NT_DIMS, preferred_element_type=F32
        )
        code_ref[...] = sent[0:1] * 256.0 + sent[1:2]
    slot_row = tag_ref[...] * capacity + rank
    for ((low_tag, high_tag), (first, last)), out_ref in zip(parts, outs):
        rows = chosen(slot_row, low_tag * capacity, high_tag * capacity)
        width = last - first
        for half in range(2):
            hi, mid, low = split3(observed_ref[:, half * bins + first : half * bins + last])
            out_ref[:, half * width : (half + 1) * width] = mm(rows, hi) + mm(rows, mid) + mm(rows, low)


def forward_kernel(
    steps, records_ref, cos_a_ref, sin_a_ref, cos_b_ref, sin_b_ref, rows_ref,
    white_ref, picked_ref, table, total,
):
    step = pl.program_id(0)
    bins = cos_b_ref.shape[1]
    parts = table.shape[0] // BASE

    @pl.when(step == 0)
    def _():
        total[...] = jnp.zeros_like(total)

    for part in range(parts):
        row = step * parts + part
        cos_a = cos_a_ref[pl.ds(row, 1), :]
        sin_a = sin_a_ref[pl.ds(row, 1), :]
        cos_b = cos_b_ref[...]
        sin_b = sin_b_ref[...]
        rows = slice(part * BASE, (part + 1) * BASE)
        table[rows, :bins] = (cos_a * cos_b - sin_a * sin_b).astype(BF16)
        table[rows, bins:] = (sin_a * cos_b + cos_a * sin_b).astype(BF16)
    total[...] += mm(records_ref[...], table[...])

    @pl.when(step == steps - 1)
    def _():
        spectra = total[...]
        power = jnp.sum(spectra * spectra, axis=1, keepdims=True) / bins
        white = spectra / jnp.sqrt(power + 1e-06)
        white_ref[...] = white
        chosen = (
            lax.broadcasted_iota(jnp.int32, (rows_ref.shape[0], white.shape[0]), 1) == rows_ref[...]
        ).astype(F32).astype(BF16)
        hi, mid, low = split3(white)
        picked_ref[...] = mm(chosen, hi) + mm(chosen, mid) + mm(chosen, low)


def pair_kernel(bins, spans, starts, count, code_ref, white_ref, sources_ref, *refs):
    blocks, begun, outs, misfit_ref = (
        refs[:count], refs[count : count + starts], refs[count + starts : -1], refs[-1],
    )
    begin = spans[0][0]
    total = spans[-1][1] - begin
    slots = code_ref.shape[1]
    rows, owners = white_ref.shape[0], sources_ref.shape[0]
    code = code_ref[...]
    receiver = code // 256 - 1
    source = code % 256
    scatter = (lax.broadcasted_iota(jnp.int32, (rows, slots), 0) == receiver).astype(F32)
    source_hits = (
        (lax.broadcasted_iota(jnp.int32, (LANES, slots), 0) == source) & (receiver >= 0)
    ).astype(F32)
    gather = scatter.T.astype(BF16)
    gather2 = jnp.concatenate([gather, gather], axis=1)
    scatter = scatter.astype(BF16)
    scatter2 = jnp.concatenate([scatter, scatter], axis=1)
    pick = source_hits.T[:, :owners].astype(BF16)

    def rows_of(left):
        hi, low = split2(white_ref[:, left : left + LANES])
        return mm(gather2, jnp.concatenate([hi, low], axis=0))

    def sources_of(left):
        hi, low = split2(sources_ref[:, left : left + LANES])
        return mm(pick, hi) + mm(pick, low)

    def summed(terms):
        hi, low = split2(terms)
        return mm(scatter2, jnp.concatenate([hi, low], axis=0))

    def seen(left):
        return jnp.concatenate([block[:, left : left + LANES] for block in blocks], axis=0)

    misfit = jnp.zeros((slots, LANES), F32)
    for number, (first, last) in enumerate(spans):
        width = last - first
        for at in range(0, width, LANES):
            lo = first + at
            index = lo + lax.broadcasted_iota(jnp.int32, (1, LANES), 1)
            weights = 0.5 - 0.5 * jnp.cos((index.astype(F32) + 0.5) * (2.0 * math.pi / bins))
            receiver_real, receiver_imag = rows_of(lo), rows_of(bins + lo)
            source_real, source_imag = sources_of(lo), sources_of(bins + lo)
            diff_real = source_real * receiver_real + source_imag * receiver_imag - seen(lo - begin)
            diff_imag = source_real * receiver_imag - source_imag * receiver_real - seen(total + lo - begin)
            residual_real = weights * diff_real
            residual_imag = weights * diff_imag
            misfit = misfit + (residual_real * diff_real + residual_imag * diff_imag)
            real = summed(residual_real * source_real - residual_imag * source_imag)
            imag = summed(residual_real * source_imag + residual_imag * source_real)
            if starts:
                real = real + begun[number][:, at : at + LANES]
                imag = imag + begun[number][:, width + at : width + at + LANES]
            outs[number][:, at : at + LANES] = real
            outs[number][:, width + at : width + at + LANES] = imag
    misfit_ref[...] = jnp.sum(misfit, axis=1, keepdims=True) / (2 * bins)


def inverse_kernel(scale, mix_ref, turn_cos_ref, turn_sin_ref, last_ref, *refs):
    chunks, (out_ref, held, wide) = refs[:-3], refs[-3:]
    count = out_ref.shape[0]
    blocks = held.shape[1] // 2
    steps = mix_ref.shape[0] // 2
    turns = turn_cos_ref.shape[0]
    at = 0
    for chunk in chunks:
        width = chunk.shape[1] // 2
        for block in range(width // LANES):
            for half in range(2):
                left = half * width + block * LANES
                held[:, half * blocks + at, :] = chunk[:, left : left + LANES]
            at += 1
    mix = mix_ref[...]
    last = last_ref[...]
    turn_cos = turn_cos_ref[...]
    turn_sin = turn_sin_ref[...]
    for row in range(count):
        hi, low = split2(held[row])
        mixed = mm(mix, jnp.concatenate([hi, low, hi], axis=0))
        real = jnp.concatenate([mixed[:steps]] * (turns // steps), axis=0)
        imag = jnp.concatenate([mixed[steps:]] * (turns // steps), axis=0)
        turned = jnp.concatenate(
            [real * turn_cos - imag * turn_sin, real * turn_sin + imag * turn_cos], axis=1
        )
        hi, low = split2(turned)
        wide[row] = lax.dot_general(
            last, jnp.concatenate([hi, low, hi], axis=1), NT_DIMS, preferred_element_type=F32
        )
    for block in range(wide.shape[1]):
        out_ref[:, block * LANES : (block + 1) * LANES] = wide[:, block, :] * scale


def bf16_parts(values):
    hi = values.astype(jnp.bfloat16)
    return hi, (values - hi.astype(np.float64)).astype(jnp.bfloat16)


def inverse(chunks, time_len, bins):
    period = 2 * time_len
    blocks = bins // LANES
    steps = period // LANES
    turns = LANES
    outer = time_len // turns
    cos, sin = phases(np.arange(steps)[:, None] * np.arange(blocks)[None, :] * LANES, period)
    mix = np.concatenate(
        [np.concatenate([cos, -sin], axis=1), np.concatenate([sin, cos], axis=1)], axis=0
    )
    hi, low = bf16_parts(mix)
    mix = np.concatenate([hi, hi, low], axis=1)
    r = np.arange(LANES)[None, :]
    turn_cos, turn_sin = phases((K0 + r) * np.arange(turns)[:, None], period)
    cos, sin = phases((K0 + r) * np.arange(outer)[:, None] * turns, period)
    hi, low = bf16_parts(np.concatenate([cos, -sin], axis=1))
    last = np.concatenate([hi, hi, low], axis=1)
    count = chunks[0].shape[0]
    return pl.pallas_call(
        functools.partial(inverse_kernel, 1.0 / math.sqrt(bins)),
        out_shape=jax.ShapeDtypeStruct((count, time_len), F32),
        in_specs=[VMEM] * (4 + len(chunks)),
        out_specs=VMEM,
        scratch_shapes=[
            pltpu.VMEM((count, 2 * blocks, LANES), F32),
            pltpu.VMEM((count, outer, LANES), F32),
        ],
        cost_estimate=pl.CostEstimate(flops=1_000_000_000, bytes_accessed=2_000_000, transcendentals=0),
        name="inverse",
    )(jnp.asarray(mix), jnp.asarray(turn_cos, F32), jnp.asarray(turn_sin, F32), jnp.asarray(last), *chunks)


def exchange(value, axis):
    return lax.all_to_all(value, axis, split_axis=0, concat_axis=0, tiled=True)


def scatter_sum(value, axis):
    size = lax.axis_size(axis)
    index = lax.axis_index(axis)
    rows, width = value.shape
    value = value.reshape(size, rows // size, width)
    bit = 1
    while bit < size:
        pairs = [(i, i ^ bit) for i in range(size)]
        blocks = value.shape[0]
        value = value.reshape(blocks // 2, 2, rows // size, width)
        side = (index // bit) % 2
        kept = lax.dynamic_index_in_dim(value, side, 1, keepdims=False)
        sent = lax.dynamic_index_in_dim(value, 1 - side, 1, keepdims=False)
        moved = lax.ppermute(sent, axis, pairs)
        value = kept + moved
        bit *= 2
    return value.reshape(rows // size, width)


def per_device(records, virtual_sources, pair_group, pair_receiver, pair_source, observed):
    row_count, time_len = records.shape
    pair_count = observed.shape[0]
    bins = observed.shape[1] // 2
    groups = lax.axis_size("chan")
    capacity = 2 * pair_count // groups
    slots = groups * capacity
    owners = virtual_sources.shape[0]
    chan_index = lax.axis_index("chan")
    routed = groups == 8
    cut = bins * CUT // 8
    spans = [(0, cut), (cut, bins)]
    full = (0, bins)
    group_row = pair_group.reshape(1, pair_count)
    lists = (
        group_row ^ chan_index if routed else group_row,
        group_row,
        pair_receiver.reshape(1, pair_count),
        pair_source.reshape(1, pair_count),
    )

    def pack(parts, labelled):
        shapes = [
            jax.ShapeDtypeStruct(((high - low) * capacity, 2 * (last - first)), F32)
            for (low, high), (first, last) in parts
        ]
        if labelled:
            shapes.append(jax.ShapeDtypeStruct((1, slots), F32))
            shapes.append(jax.ShapeDtypeStruct((1, pair_count), jnp.int32))
        return pl.pallas_call(
            functools.partial(pack_kernel, parts, groups),
            out_shape=shapes,
            in_specs=[VMEM] * 5,
            out_specs=[VMEM] * len(shapes),
            cost_estimate=pl.CostEstimate(flops=400_000_000, bytes_accessed=3_000_000, transcendentals=0),
            name="pack",
        )(*lists, observed)

    def move(value, tag):
        return lax.ppermute(value, "chan", [(i, i ^ tag) for i in range(groups)])

    early = {}
    if routed:
        *sent, code, slot = pack([((tag, tag + 1), full) for tag in FIRST], True)
        for tag, value in zip(FIRST, sent):
            early[tag] = move(value, tag)
        own, middle, last_a, last_b = pack(
            [((0, 1), full), ((MIDDLE, MIDDLE + 1), full)]
            + [((LAST, LAST + 1), span) for span in spans],
            False,
        )
    else:
        own, code, slot = pack([((0, groups), full)], True)

    period = 2 * time_len
    k = K0 + np.arange(bins)[None, :]
    cos_a, sin_a = phases(k * BASE * np.arange(time_len // BASE)[:, None], period)
    cos_b, sin_b = phases(k * np.arange(BASE)[:, None], period)
    steps = 8
    block = time_len // steps
    whole = lambda shape: pl.BlockSpec(shape, lambda i: (0, 0))
    whitened, picked = pl.pallas_call(
        functools.partial(forward_kernel, steps),
        grid=(steps,),
        out_shape=[
            jax.ShapeDtypeStruct((row_count, 2 * bins), F32),
            jax.ShapeDtypeStruct((owners, 2 * bins), F32),
        ],
        in_specs=[
            pl.BlockSpec((row_count, block), lambda i: (0, i)),
            whole(cos_a.shape), whole(cos_a.shape), whole(cos_b.shape), whole(cos_b.shape),
            whole((owners, 1)),
        ],
        out_specs=[whole((row_count, 2 * bins)), whole((owners, 2 * bins))],
        scratch_shapes=[pltpu.VMEM((block, 2 * bins), BF16), pltpu.VMEM((row_count, 2 * bins), F32)],
        cost_estimate=pl.CostEstimate(flops=8_000_000_000, bytes_accessed=4_000_000, transcendentals=0),
        name="forward",
    )(
        records, jnp.asarray(cos_a, F32), jnp.asarray(-sin_a, F32), jnp.asarray(cos_b, F32),
        jnp.asarray(-sin_b, F32), (virtual_sources - chan_index * row_count).reshape(owners, 1),
    )

    part = 2 * bins // groups
    spread = picked.reshape(owners, groups, part).transpose(1, 0, 2)
    label = jnp.pad(code.reshape(groups, 1, capacity), ((0, 0), (0, 7), (0, part - capacity)))
    arrived = exchange(jnp.concatenate([spread, label], axis=1), "chan")
    order = chan_index ^ jnp.arange(groups, dtype=jnp.int32) if routed else None
    codes = arrived[:, owners, :capacity].astype(jnp.int32)
    codes = jnp.take(codes, order, axis=0) if routed else codes
    summed = jnp.sum(arrived[:, :owners], axis=0)
    sources = exchange(jnp.broadcast_to(summed[None], (groups, owners, part)), "chan")
    sources = sources.transpose(1, 0, 2).reshape(owners, 2 * bins)

    def terms(blocks, which, some, begun):
        chosen = codes.reshape(1, slots)
        if routed:
            chosen = jnp.concatenate([codes[tag] for tag in which]).reshape(1, -1)
        count = chosen.shape[1]
        *sums, misfit = pl.pallas_call(
            functools.partial(pair_kernel, bins, some, len(begun), len(blocks)),
            out_shape=[jax.ShapeDtypeStruct((row_count, 2 * (last - first)), F32) for first, last in some]
            + [jax.ShapeDtypeStruct((count, 1), F32)],
            in_specs=[VMEM] * (3 + len(blocks) + len(begun)),
            out_specs=[VMEM] * (len(some) + 1),
            cost_estimate=pl.CostEstimate(flops=2_000_000_000, bytes_accessed=5_000_000, transcendentals=0),
            name="pairs",
        )(chosen, whitened, sources, *blocks, *begun)
        return sums, misfit.reshape(-1, capacity)

    if routed:
        middle = move(middle, MIDDLE)
        last_a = move(last_a, LAST)
        last_b = move(last_b, LAST)
        tags = [0, *FIRST, MIDDLE]
        sums, misfit = terms([own, *early.values(), middle], tags, spans, [])
        (sum_a,), misfit_a = terms([last_a], [LAST], spans[:1], sums[:1])
        spectra = [scatter_sum(sum_a, "src")]
        (sum_b,), misfit_b = terms([last_b], [LAST], spans[1:], sums[1:])
        spectra.append(scatter_sum(sum_b, "src"))
        misfit = jnp.concatenate([misfit, misfit_a + misfit_b], axis=0)
        place = np.argsort(np.array([*tags, LAST]))
        misfit = jnp.take(misfit, jnp.asarray(place)[order], axis=0)
    else:
        sums, misfit = terms([exchange(own.reshape(groups, capacity, -1), "chan").reshape(slots, -1)], [], spans, [])
        spectra = [scatter_sum(value, "src") for value in sums]

    returned = exchange(misfit, "chan").reshape(slots, 1)
    hits = lax.broadcasted_iota(jnp.int32, (slots, pair_count), 0) == slot
    pair_misfit = jnp.sum(jnp.where(hits, returned, 0.0), axis=0)
    result = inverse(spectra, time_len, bins)
    return (result, pair_misfit)


def solution(mesh):
    return jax.shard_map(
        per_device,
        mesh=mesh,
        in_specs=(
            P("chan", None),
            P("src"),
            P(("chan", "src"), None),
            P(("chan", "src")),
            P(("chan", "src")),
            P(("chan", "src"), None),
        ),
        out_specs=(P(("chan", "src"), None), P(("chan", "src"))),
        check_vma=False,
    )
```

```python
import functools
import math

import jax
import jax.numpy as jnp
import numpy as np
from jax import lax
from jax.experimental import pallas as pl
from jax.experimental.pallas import tpu as pltpu
from jax.sharding import PartitionSpec as P


K0 = 64
LANES = 128
CUT = 6
GRANT = pltpu.CompilerParams(vmem_limit_bytes=12 * 1024 * 1024)
FIRST = (6,)
SECOND = (7,)
THIRD = (2, 3, 1)
LATE = (4,)
LAST = 5
EARLY = [0, *FIRST, *SECOND, *THIRD]
BASE = 64
F32 = jnp.float32
BF16 = jnp.bfloat16
VMEM = pl.BlockSpec(memory_space=pltpu.VMEM)
NT_DIMS = (((1,), (1,)), ((), ()))


def mm(a, b):
    return jnp.dot(a, b, preferred_element_type=F32)


def split2(x):
    hi = x.astype(BF16)
    return hi, (x - hi.astype(F32)).astype(BF16)


def split3(x):
    hi = x.astype(BF16)
    rest = x - hi.astype(F32)
    mid = rest.astype(BF16)
    return hi, mid, (rest - mid.astype(F32)).astype(BF16)


def phases(products, period):
    angles = (products % period) * (2.0 * math.pi / period)
    return np.cos(angles), np.sin(angles)


def pack_kernel(parts, groups, here_ref, group_ref, receiver_ref, source_ref, observed_ref, *outs):
    pairs = observed_ref.shape[0]
    bins = observed_ref.shape[1] // 2
    capacity = 2 * pairs // groups
    group_row = group_ref[...]
    hits = (
        lax.broadcasted_iota(jnp.int32, (max(groups, 8), pairs), 0) == group_row
    ).astype(F32)
    earlier = (
        lax.broadcasted_iota(jnp.int32, (pairs, pairs), 0)
        < lax.broadcasted_iota(jnp.int32, (pairs, pairs), 1)
    ).astype(F32)
    counts = mm(hits.astype(BF16), earlier.astype(BF16))
    rank = jnp.sum(hits * counts, axis=0, keepdims=True).astype(jnp.int32)

    def chosen(slot_row, start, stop):
        index = start + lax.broadcasted_iota(jnp.int32, (stop - start, pairs), 0)
        return (index == slot_row).astype(F32).astype(BF16)

    if len(outs) > len(parts):
        label_ref, slot_ref = outs[-2:]
        slot_row = group_row * capacity + rank
        slot_ref[...] = slot_row
        labels = jnp.concatenate(
            [receiver_ref[...] + 1, source_ref[...]] + [jnp.zeros((6, pairs), jnp.int32)], axis=0
        ).astype(F32).astype(BF16)
        sent = lax.dot_general(
            labels, chosen(slot_row, 0, groups * capacity), NT_DIMS, preferred_element_type=F32
        )
        code = jnp.broadcast_to(sent[0:1] * 256.0 + sent[1:2], (8, groups * capacity))
        label_ref[...] = jnp.zeros_like(label_ref)
        for group in range(groups):
            label_ref[group, :, :capacity] = code[:, group * capacity : (group + 1) * capacity]
    slot_row = (group_row ^ here_ref[0, 0]) * capacity + rank
    for span in dict.fromkeys(part[1] for part in parts):
        mine = [(tags, ref) for (tags, other), ref in zip(parts, outs) if other == span]
        rows = jnp.concatenate(
            [chosen(slot_row, low * capacity, high * capacity) for (low, high), _ in mine], axis=0
        )
        rows = jnp.concatenate([rows] * 3, axis=1)
        width = span[1] - span[0]
        tile = math.gcd(width, 256)
        for half in range(2):
            for at in range(0, width, tile):
                left = half * bins + span[0] + at
                values = mm(rows, jnp.concatenate(split3(observed_ref[:, left : left + tile]), axis=0))
                top = 0
                for (low, high), out_ref in mine:
                    count = (high - low) * capacity
                    out_ref[:, half * width + at : half * width + at + tile] = values[top : top + count]
                    top += count


def forward_kernel(
    steps, records_ref, cos_a_ref, sin_a_ref, cos_b_ref, sin_b_ref, rows_ref, label_ref,
    white_ref, picked_ref, table, total,
):
    step = pl.program_id(0)
    bins = cos_b_ref.shape[1]
    parts = table.shape[0] // BASE

    @pl.when(step == 0)
    def _():
        total[...] = jnp.zeros_like(total)

    for part in range(parts):
        row = step * parts + part
        cos_a = cos_a_ref[pl.ds(row, 1), :]
        sin_a = sin_a_ref[pl.ds(row, 1), :]
        cos_b = cos_b_ref[...]
        sin_b = sin_b_ref[...]
        rows = slice(part * BASE, (part + 1) * BASE)
        table[rows, :bins] = (cos_a * cos_b - sin_a * sin_b).astype(BF16)
        table[rows, bins:] = (sin_a * cos_b + cos_a * sin_b).astype(BF16)
    total[...] += mm(records_ref[...], table[...])

    @pl.when(step == steps - 1)
    def _():
        spectra = total[...]
        power = jnp.sum(spectra * spectra, axis=1, keepdims=True) / bins
        white = spectra / jnp.sqrt(power + 1e-06)
        white_ref[...] = white
        owners = rows_ref.shape[0]
        chosen = (
            lax.broadcasted_iota(jnp.int32, (owners, white.shape[0]), 1) == rows_ref[...]
        ).astype(F32).astype(BF16)
        picked = mm(jnp.concatenate([chosen] * 3, axis=1), jnp.concatenate(split3(white), axis=0))
        part = picked_ref.shape[2]
        for group in range(picked_ref.shape[0]):
            picked_ref[group, :owners, :] = picked[:, group * part : (group + 1) * part]
        picked_ref[:, owners:, :] = label_ref[...]


def spread_kernel(arrived_ref, out_ref):
    owners = out_ref.shape[1]
    summed = arrived_ref[0, :owners, :]
    for group in range(1, arrived_ref.shape[0]):
        summed = summed + arrived_ref[group, :owners, :]
    out_ref[...] = jnp.broadcast_to(summed[None], out_ref.shape)


def pair_kernel(
    bins, spans, tags, whole_block, starts, older, last_of, split, here_ref, arrived_ref, white_ref, sources_ref, *refs
):
    count = 1 if whole_block else len(tags)
    pieces = split
    refs = list(refs)
    blocks, begun = refs[:count], refs[count : count + starts]
    before = refs[count + starts : count + starts + len(older)]
    refs = refs[count + starts + len(older) :]
    outs, misfits = refs[: sum(pieces)], refs[sum(pieces) :]
    begin = spans[0][0]
    total = spans[-1][1] - begin
    rows = white_ref.shape[0]
    _, owners, part = sources_ref.shape
    capacity = misfits[0].shape[1]
    here, side = here_ref[0, 0], here_ref[0, 1]
    quarter = rows // 4
    gathers, picks = [], []
    for tag in tags:
        code = arrived_ref[tag if whole_block else here ^ tag, owners : owners + 8, :capacity]
        code = code[0:1, :].astype(jnp.int32)
        receiver = code // 256 - 1
        source = code % 256
        hit = (lax.broadcasted_iota(jnp.int32, (rows, capacity), 0) == receiver).astype(F32)
        gathers.append(hit.T)
        hit = (
            (lax.broadcasted_iota(jnp.int32, (LANES, capacity), 0) == source) & (receiver >= 0)
        ).astype(F32)
        picks.append(hit.T)
    gather = jnp.concatenate(gathers, axis=0)
    pick = jnp.concatenate(picks, axis=0).astype(BF16)
    place = lax.broadcasted_iota(jnp.int32, (rows, rows), 0)
    block = place // quarter
    block = (((block & 1) << 1) | (block >> 1)) ^ side
    wanted = block * quarter + place % quarter
    order = (lax.broadcasted_iota(jnp.int32, (rows, rows), 1) == wanted).astype(F32).astype(BF16)
    gather2 = gather.astype(BF16)
    scatter = lax.dot_general(order, gather2, NT_DIMS, preferred_element_type=F32).astype(BF16)
    gather2 = jnp.concatenate([gather2, gather2], axis=1)
    scatter2 = jnp.concatenate([scatter, scatter], axis=1)
    slots = gather.shape[0]
    tile = 2 * LANES if all((last - first) % (2 * LANES) == 0 for first, last in spans) else LANES

    def rows_of(left):
        hi, low = split2(white_ref[:, left : left + tile])
        return mm(gather2, jnp.concatenate([hi, low], axis=0))

    def sources_of(left):
        taken = min(tile, part)
        values = jnp.concatenate(
            [sources_ref[at // part, :, at % part : at % part + taken] for at in range(left, left + tile, taken)],
            axis=1,
        )
        values = jnp.concatenate([values, jnp.zeros((LANES - owners, tile), F32)], axis=0)
        hi, low = split2(values)
        return mm(jnp.concatenate([pick, pick], axis=1), jnp.concatenate([hi, low], axis=0))

    def summed(terms):
        hi, low = split2(terms)
        return mm(scatter2, jnp.concatenate([hi, low], axis=0))

    def seen(half, lo):
        values = []
        for block in blocks:
            left = half * bins + lo if block.shape[1] == 2 * bins else half * total + lo - begin
            values.append(block[:, left : left + tile])
        return jnp.concatenate(values, axis=0)

    misfit = jnp.zeros((slots, tile), F32)
    for number, (first, last) in enumerate(spans):
        width = last - first
        mine = outs[sum(pieces[:number]) : sum(pieces[: number + 1])]

        def put(left, value):
            if starts:
                value = value + begun[number][:, left : left + tile]
            size = rows // len(mine)
            for piece, ref in enumerate(mine):
                ref[:, left : left + tile] = value[piece * size : (piece + 1) * size]

        for at in range(0, width, tile):
            lo = first + at
            index = lo + lax.broadcasted_iota(jnp.int32, (1, tile), 1)
            weights = 0.5 - 0.5 * jnp.cos((index.astype(F32) + 0.5) * (2.0 * math.pi / bins))
            receiver_real, receiver_imag = rows_of(lo), rows_of(bins + lo)
            source_real, source_imag = sources_of(lo), sources_of(bins + lo)
            diff_real = source_real * receiver_real + source_imag * receiver_imag - seen(0, lo)
            diff_imag = source_real * receiver_imag - source_imag * receiver_real - seen(1, lo)
            residual_real = weights * diff_real
            residual_imag = weights * diff_imag
            misfit = misfit + (residual_real * diff_real + residual_imag * diff_imag)
            put(at, summed(residual_real * source_real - residual_imag * source_imag))
            put(width + at, summed(residual_real * source_imag + residual_imag * source_real))
    misfit = jnp.sum(misfit, axis=1, keepdims=True) / (2 * bins)
    index = lax.broadcasted_iota(jnp.int32, (slots, capacity), 0) % capacity
    spots = lax.broadcasted_iota(jnp.int32, (slots, capacity), 1)
    spread = jnp.where(index == spots, misfit, 0.0)
    found = [
        jnp.sum(spread[number * capacity : (number + 1) * capacity], axis=0, keepdims=True)
        for number in range(len(tags))
    ]
    (misfit_ref,) = misfits
    if not last_of:
        for number in range(len(tags)):
            misfit_ref[number : number + 1, :] = found[number]
        return
    for ref, names in zip(before, older):
        for number, tag in enumerate(names):
            value = ref[number : number + 1, :]
            if tag in tags:
                found[tags.index(tag)] = found[tags.index(tag)] + value
            else:
                misfit_ref[pl.ds(here ^ tag, 1), :] = value
    for number, tag in enumerate(tags):
        misfit_ref[pl.ds(tag if whole_block else here ^ tag, 1), :] = found[number]


def looked(returned, slot):
    groups, capacity = returned.shape
    pairs = slot.shape[1]
    group = (
        lax.broadcasted_iota(jnp.int32, (groups, pairs), 0) == slot // capacity
    ).astype(F32).astype(BF16)
    parts = split3(returned.T)
    values = mm(parts[0], group) + mm(parts[1], group) + mm(parts[2], group)
    rank = lax.broadcasted_iota(jnp.int32, (capacity, pairs), 0) == slot % capacity
    return jnp.sum(jnp.where(rank, values, 0.0), axis=0, keepdims=True)


def inverse_kernel(
    scale, sizes, mix_ref, turn_cos_ref, turn_sin_ref, last_ref, slot_ref, returned_ref, *refs
):
    chunks = refs[: sum(sizes)]
    out_ref, misfit_ref, held, wide = refs[-4:]
    misfit_ref[...] = looked(returned_ref[...], slot_ref[...])
    count = out_ref.shape[0]
    blocks = held.shape[1] // 2
    steps = mix_ref.shape[0] // 2
    turns = turn_cos_ref.shape[0]
    at = 0
    for number, size in enumerate(sizes):
        addends = chunks[sum(sizes[:number]) : sum(sizes[: number + 1])]
        width = addends[0].shape[1] // 2
        for block in range(width // LANES):
            for half in range(2):
                left = half * width + block * LANES
                value = addends[0][:count, left : left + LANES]
                for other in addends[1:]:
                    value = value + other[:count, left : left + LANES]
                held[:, half * blocks + at, :] = value
            at += 1
    mix = mix_ref[...]
    last = last_ref[...]
    turn_cos = turn_cos_ref[...]
    turn_sin = turn_sin_ref[...]
    for row in range(count):
        hi, low = split2(held[row])
        mixed = mm(mix, jnp.concatenate([hi, low, hi], axis=0))
        real = jnp.concatenate([mixed[:steps]] * (turns // steps), axis=0)
        imag = jnp.concatenate([mixed[steps:]] * (turns // steps), axis=0)
        turned = jnp.concatenate(
            [real * turn_cos - imag * turn_sin, real * turn_sin + imag * turn_cos], axis=1
        )
        hi, low = split2(turned)
        wide[row] = lax.dot_general(
            last, jnp.concatenate([hi, low, hi], axis=1), NT_DIMS, preferred_element_type=F32
        )
    for block in range(wide.shape[1]):
        out_ref[:, block * LANES : (block + 1) * LANES] = wide[:, block, :] * scale


def bf16_parts(values):
    hi = values.astype(jnp.bfloat16)
    return hi, (values - hi.astype(np.float64)).astype(jnp.bfloat16)


def inverse(slot, returned, spectra, count, time_len, bins):
    period = 2 * time_len
    blocks = bins // LANES
    steps = period // LANES
    turns = LANES
    outer = time_len // turns
    cos, sin = phases(np.arange(steps)[:, None] * np.arange(blocks)[None, :] * LANES, period)
    mix = np.concatenate(
        [np.concatenate([cos, -sin], axis=1), np.concatenate([sin, cos], axis=1)], axis=0
    )
    hi, low = bf16_parts(mix)
    mix = np.concatenate([hi, hi, low], axis=1)
    r = np.arange(LANES)[None, :]
    turn_cos, turn_sin = phases((K0 + r) * np.arange(turns)[:, None], period)
    cos, sin = phases((K0 + r) * np.arange(outer)[:, None] * turns, period)
    hi, low = bf16_parts(np.concatenate([cos, -sin], axis=1))
    last = np.concatenate([hi, hi, low], axis=1)
    chunks = [value for addends in spectra for value in addends]
    sizes = [len(addends) for addends in spectra]
    return pl.pallas_call(
        functools.partial(inverse_kernel, 1.0 / math.sqrt(bins), sizes),
        out_shape=[jax.ShapeDtypeStruct((count, time_len), F32), jax.ShapeDtypeStruct(slot.shape, F32)],
        in_specs=[VMEM] * (6 + len(chunks)),
        out_specs=[VMEM] * 2,
        scratch_shapes=[
            pltpu.VMEM((count, 2 * blocks, LANES), F32),
            pltpu.VMEM((count, outer, LANES), F32),
        ],
        compiler_params=GRANT,
        cost_estimate=pl.CostEstimate(flops=1_000_000_000, bytes_accessed=2_000_000, transcendentals=0),
        name="inverse",
    )(
        in_hbm(mix), in_hbm(np.float32(turn_cos)), in_hbm(np.float32(turn_sin)), in_hbm(last),
        slot, returned, *chunks,
    )


def in_hbm(value):
    return pltpu.with_memory_space_constraint(jnp.asarray(value), pltpu.HBM)


def exchange(value, axis):
    return lax.all_to_all(value, axis, split_axis=0, concat_axis=0, tiled=True)


def over_src(value, step):
    return lax.ppermute(value, "src", [(i, i ^ step) for i in range(4)])


def rows_in_two(kept, sent):
    half = kept.shape[0] // 2
    moved = over_src(sent, 1)
    return [kept, moved, over_src(kept[half:] + moved[half:], 2)]


def rows_in_one(own, *others):
    return [own] + [over_src(value, step) for value, step in zip(others, (2, 1, 3))]


def per_device(records, virtual_sources, pair_group, pair_receiver, pair_source, observed):
    row_count, time_len = records.shape
    pair_count = observed.shape[0]
    bins = observed.shape[1] // 2
    groups = lax.axis_size("chan")
    assert lax.axis_size("src") == 4
    capacity = 2 * pair_count // groups
    slots = groups * capacity
    owners = virtual_sources.shape[0]
    chan_index = lax.axis_index("chan")
    routed = groups == 8
    part = 2 * bins // groups
    cut = bins * CUT // 8
    spans = [(0, cut), (cut, bins)]
    full = (0, bins)
    here = jnp.stack([chan_index if routed else 0 * chan_index, lax.axis_index("src")]).reshape(1, 2)
    smem = pl.BlockSpec(memory_space=pltpu.SMEM)
    lists = (
        here,
        in_hbm(pair_group.reshape(1, pair_count)),
        in_hbm(pair_receiver.reshape(1, pair_count)),
        in_hbm(pair_source.reshape(1, pair_count)),
    )

    def pack(parts, labelled):
        shapes = [
            jax.ShapeDtypeStruct(((high - low) * capacity, 2 * (last - first)), F32)
            for (low, high), (first, last) in parts
        ]
        if labelled:
            shapes.append(jax.ShapeDtypeStruct((groups, 8, part), F32))
            shapes.append(jax.ShapeDtypeStruct((1, pair_count), jnp.int32))
        return pl.pallas_call(
            functools.partial(pack_kernel, parts, groups),
            out_shape=shapes,
            in_specs=[smem] + [VMEM] * 4,
            out_specs=[VMEM] * len(shapes),
            compiler_params=GRANT,
            cost_estimate=pl.CostEstimate(flops=400_000_000, bytes_accessed=3_000_000, transcendentals=0),
            name="pack",
        )(*lists, observed)

    def move(value, tag):
        return lax.ppermute(value, "chan", [(i, i ^ tag) for i in range(groups)])

    if routed:
        *sent, label, slot = pack([((tag, tag + 1), full) for tag in FIRST], True)
        blocks = {tag: move(value, tag) for tag, value in zip(FIRST, sent)}
        rest = [*SECOND, *THIRD, *LATE]
        *sent, last_a, last_b, blocks[0] = pack(
            [((tag, tag + 1), full) for tag in rest]
            + [((LAST, LAST + 1), span) for span in spans]
            + [((0, 1), full)],
            False,
        )
    else:
        own, label, slot = pack([((0, groups), full)], True)

    period = 2 * time_len
    k = K0 + np.arange(bins)[None, :]
    cos_a, sin_a = phases(k * BASE * np.arange(time_len // BASE)[:, None], period)
    cos_b, sin_b = phases(k * np.arange(BASE)[:, None], period)
    steps = 8
    block = time_len // steps
    whole = lambda *shape: pl.BlockSpec(shape, lambda i: (0,) * len(shape))
    whitened, picked = pl.pallas_call(
        functools.partial(forward_kernel, steps),
        grid=(steps,),
        out_shape=[
            jax.ShapeDtypeStruct((row_count, 2 * bins), F32),
            jax.ShapeDtypeStruct((groups, owners + 8, part), F32),
        ],
        in_specs=[
            pl.BlockSpec((row_count, block), lambda i: (0, i)),
            whole(*cos_a.shape), whole(*cos_a.shape), whole(*cos_b.shape), whole(*cos_b.shape),
            whole(owners, 1), whole(groups, 8, part),
        ],
        out_specs=[whole(row_count, 2 * bins), whole(groups, owners + 8, part)],
        scratch_shapes=[pltpu.VMEM((block, 2 * bins), BF16), pltpu.VMEM((row_count, 2 * bins), F32)],
        compiler_params=GRANT,
        cost_estimate=pl.CostEstimate(flops=8_000_000_000, bytes_accessed=4_000_000, transcendentals=0),
        name="forward",
    )(
        records, in_hbm(np.float32(cos_a)), in_hbm(np.float32(-sin_a)), in_hbm(np.float32(cos_b)),
        in_hbm(np.float32(-sin_b)), (virtual_sources - chan_index * row_count).reshape(owners, 1), label,
    )

    arrived = exchange(picked, "chan")
    summed = pl.pallas_call(
        spread_kernel,
        out_shape=jax.ShapeDtypeStruct((groups, owners, part), F32),
        in_specs=[VMEM],
        out_specs=VMEM,
        compiler_params=GRANT,
        cost_estimate=pl.CostEstimate(flops=100_000, bytes_accessed=300_000, transcendentals=0),
        name="spread",
    )(arrived)
    sources = exchange(summed, "chan")

    def terms(values, tags, some, split, begun, before, older=(), last_of=False):
        shapes = [
            jax.ShapeDtypeStruct((row_count // pieces, 2 * (last - first)), F32)
            for (first, last), pieces in zip(some, split)
            for _ in range(pieces)
        ] + [jax.ShapeDtypeStruct((groups if last_of else len(tags), capacity), F32)]
        return pl.pallas_call(
            functools.partial(
                pair_kernel, bins, some, tags, not routed, len(begun), older, last_of, split
            ),
            out_shape=shapes,
            in_specs=[smem] + [VMEM] * (3 + len(values) + len(begun) + len(before)),
            out_specs=[VMEM] * len(shapes),
            compiler_params=GRANT,
            cost_estimate=pl.CostEstimate(flops=2_000_000_000, bytes_accessed=5_000_000, transcendentals=0),
            name="pairs",
        )(here, arrived, whitened, sources, *values, *begun, *before)

    if routed:
        for tag, value in zip(rest, sent):
            blocks[tag] = move(value, tag)
        last_a = move(last_a, LAST)
        last_b = move(last_b, LAST)
        *begun, misfit = terms([blocks[tag] for tag in EARLY], EARLY, spans, (1, 1), [], [])
        older, before = [EARLY], [misfit]
        tags = [*LATE, LAST]
        late = [blocks[tag] for tag in LATE]
        *sums, misfit = terms([*late, last_a], tags, spans[:1], (2,), begun[:1], [])
        older.append(tags)
        before.append(misfit)
        spectra = [rows_in_two(*sums)]
        *sums, misfit = terms([*late, last_b], tags, spans[1:], (4,), begun[1:], before, older, True)
        spectra.append(rows_in_one(*sums))
    else:
        came = exchange(own.reshape(groups, capacity, -1), "chan").reshape(slots, -1)
        *sums, misfit = terms([came], list(range(groups)), spans, (2, 2), [], [], (), True)
        spectra = [rows_in_two(*sums[:2]), rows_in_two(*sums[2:])]

    returned = exchange(misfit, "chan")
    result, pair_misfit = inverse(slot, returned, spectra, row_count // 4, time_len, bins)
    return (result, pair_misfit.reshape(pair_count))


def solution(mesh):
    return jax.shard_map(
        per_device,
        mesh=mesh,
        in_specs=(
            P("chan", None),
            P("src"),
            P(("chan", "src"), None),
            P(("chan", "src")),
            P(("chan", "src")),
            P(("chan", "src"), None),
        ),
        out_specs=(P(("chan", "src"), None), P(("chan", "src"))),
        check_vma=False,
    )
```

```python
import functools
import math

import jax
import jax.numpy as jnp
import numpy as np
from jax import lax
from jax.experimental import pallas as pl
from jax.experimental.pallas import tpu as pltpu
from jax.sharding import PartitionSpec as P


K0 = 64
LANES = 128
CUT = 5
TOGETHER = 2
GRANT = pltpu.CompilerParams(vmem_limit_bytes=12 * 1024 * 1024)
FIRST = (5,)
SECOND = (6,)
THIRD = (2, 3, 1)
LATE = (7,)
LAST = 4
EARLY = [0, *FIRST, *SECOND, *THIRD]
BASE = 64
F32 = jnp.float32
BF16 = jnp.bfloat16
VMEM = pl.BlockSpec(memory_space=pltpu.VMEM)
NT_DIMS = (((1,), (1,)), ((), ()))


def mm(a, b):
    return jnp.dot(a, b, preferred_element_type=F32)


def split2(x):
    hi = x.astype(BF16)
    return hi, (x - hi.astype(F32)).astype(BF16)


def split3(x):
    hi = x.astype(BF16)
    rest = x - hi.astype(F32)
    mid = rest.astype(BF16)
    return hi, mid, (rest - mid.astype(F32)).astype(BF16)


def phases(products, period):
    angles = (products % period) * (2.0 * math.pi / period)
    return np.cos(angles), np.sin(angles)


def pack_kernel(parts, groups, here_ref, group_ref, receiver_ref, source_ref, observed_ref, *outs):
    pairs = observed_ref.shape[0]
    bins = observed_ref.shape[1] // 2
    capacity = 2 * pairs // groups
    group_row = group_ref[...]
    hits = (
        lax.broadcasted_iota(jnp.int32, (max(groups, 8), pairs), 0) == group_row
    ).astype(F32)
    earlier = (
        lax.broadcasted_iota(jnp.int32, (pairs, pairs), 0)
        < lax.broadcasted_iota(jnp.int32, (pairs, pairs), 1)
    ).astype(F32)
    counts = mm(hits.astype(BF16), earlier.astype(BF16))
    rank = jnp.sum(hits * counts, axis=0, keepdims=True).astype(jnp.int32)

    def chosen(slot_row, start, stop):
        index = start + lax.broadcasted_iota(jnp.int32, (stop - start, pairs), 0)
        return (index == slot_row).astype(F32).astype(BF16)

    if len(outs) > len(parts):
        label_ref, slot_ref = outs[-2:]
        slot_row = group_row * capacity + rank
        slot_ref[...] = slot_row
        labels = jnp.concatenate(
            [receiver_ref[...] + 1, source_ref[...]] + [jnp.zeros((6, pairs), jnp.int32)], axis=0
        ).astype(F32).astype(BF16)
        sent = lax.dot_general(
            labels, chosen(slot_row, 0, groups * capacity), NT_DIMS, preferred_element_type=F32
        )
        code = jnp.broadcast_to(sent[0:1] * 256.0 + sent[1:2], (8, groups * capacity))
        label_ref[...] = jnp.zeros_like(label_ref)
        for group in range(groups):
            label_ref[group, :, :capacity] = code[:, group * capacity : (group + 1) * capacity]
    slot_row = (group_row ^ here_ref[0, 0]) * capacity + rank
    for span in dict.fromkeys(part[1] for part in parts):
        mine = [(tags, ref) for (tags, other), ref in zip(parts, outs) if other == span]
        rows = jnp.concatenate(
            [chosen(slot_row, low * capacity, high * capacity) for (low, high), _ in mine], axis=0
        )
        rows = jnp.concatenate([rows] * 3, axis=1)
        width = span[1] - span[0]
        tile = math.gcd(width, 256)
        for half in range(2):
            for at in range(0, width, tile):
                left = half * bins + span[0] + at
                values = mm(rows, jnp.concatenate(split3(observed_ref[:, left : left + tile]), axis=0))
                top = 0
                for (low, high), out_ref in mine:
                    count = (high - low) * capacity
                    out_ref[:, half * width + at : half * width + at + tile] = values[top : top + count]
                    top += count


def forward_kernel(
    steps, records_ref, cos_a_ref, sin_a_ref, cos_b_ref, sin_b_ref, rows_ref, label_ref,
    white_ref, picked_ref, table_real, table_imag, total,
):
    step = pl.program_id(0)
    width = cos_b_ref.shape[1]
    bins = steps * width
    cos_b, sin_b = cos_b_ref[...], sin_b_ref[...]
    for row in range(cos_a_ref.shape[0]):
        cos_a, sin_a = cos_a_ref[row : row + 1, :], sin_a_ref[row : row + 1, :]
        rows = slice(row * BASE, (row + 1) * BASE)
        table_real[rows, :] = (cos_a * cos_b - sin_a * sin_b).astype(BF16)
        table_imag[rows, :] = (sin_a * cos_b + cos_a * sin_b).astype(BF16)
    left = pl.multiple_of(step * width, width)
    total[:, pl.ds(left, width)] = mm(records_ref[...], table_real[...])
    total[:, pl.ds(bins + left, width)] = mm(records_ref[...], table_imag[...])

    @pl.when(step == steps - 1)
    def _():
        spectra = total[...]
        power = jnp.sum(spectra * spectra, axis=1, keepdims=True) / bins
        white = spectra / jnp.sqrt(power + 1e-06)
        white_ref[...] = white
        owners = rows_ref.shape[0]
        chosen = (
            lax.broadcasted_iota(jnp.int32, (owners, white.shape[0]), 1) == rows_ref[...]
        ).astype(F32).astype(BF16)
        picked = mm(jnp.concatenate([chosen] * 3, axis=1), jnp.concatenate(split3(white), axis=0))
        part = picked_ref.shape[2]
        for group in range(picked_ref.shape[0]):
            picked_ref[group, :owners, :] = picked[:, group * part : (group + 1) * part]
        picked_ref[:, owners:, :] = label_ref[...]


def spread_kernel(arrived_ref, out_ref):
    owners = out_ref.shape[1]
    summed = arrived_ref[0, :owners, :]
    for group in range(1, arrived_ref.shape[0]):
        summed = summed + arrived_ref[group, :owners, :]
    out_ref[...] = jnp.broadcast_to(summed[None], out_ref.shape)


def pair_kernel(
    bins, spans, tags, whole_block, starts, older, last_of, split, here_ref, arrived_ref, white_ref, sources_ref, *refs
):
    count = 1 if whole_block else len(tags)
    pieces = split
    refs = list(refs)
    blocks, begun = refs[:count], refs[count : count + starts]
    before = refs[count + starts : count + starts + len(older)]
    refs = refs[count + starts + len(older) :]
    outs, misfits = refs[: sum(pieces)], refs[sum(pieces) :]
    begin = spans[0][0]
    total = spans[-1][1] - begin
    rows = white_ref.shape[0]
    _, owners, part = sources_ref.shape
    capacity = misfits[0].shape[1]
    here, side = here_ref[0, 0], here_ref[0, 1]
    quarter = rows // 4
    gathers, picks = [], []
    for tag in tags:
        code = arrived_ref[tag if whole_block else here ^ tag, owners : owners + 8, :capacity]
        code = code[0:1, :].astype(jnp.int32)
        receiver = code // 256 - 1
        source = code % 256
        hit = (lax.broadcasted_iota(jnp.int32, (rows, capacity), 0) == receiver).astype(F32)
        gathers.append(hit.T)
        hit = (
            (lax.broadcasted_iota(jnp.int32, (LANES, capacity), 0) == source) & (receiver >= 0)
        ).astype(F32)
        picks.append(hit.T)
    gather = jnp.concatenate(gathers, axis=0)
    pick = jnp.concatenate(picks, axis=0).astype(BF16)
    place = lax.broadcasted_iota(jnp.int32, (rows, rows), 0)
    block = place // quarter
    block = (((block & 1) << 1) | (block >> 1)) ^ side
    wanted = block * quarter + place % quarter
    order = (lax.broadcasted_iota(jnp.int32, (rows, rows), 1) == wanted).astype(F32).astype(BF16)
    gather2 = gather.astype(BF16)
    scatter = lax.dot_general(order, gather2, NT_DIMS, preferred_element_type=F32).astype(BF16)
    gather2 = jnp.concatenate([gather2, gather2], axis=1)
    scatter2 = jnp.concatenate([scatter, scatter], axis=1)
    slots = gather.shape[0]
    tile = 2 * LANES if all((last - first) % (2 * LANES) == 0 for first, last in spans) else LANES

    def rows_of(left):
        hi, low = split2(white_ref[:, left : left + tile])
        return mm(gather2, jnp.concatenate([hi, low], axis=0))

    def sources_of(left):
        taken = min(tile, part)
        values = jnp.concatenate(
            [sources_ref[at // part, :, at % part : at % part + taken] for at in range(left, left + tile, taken)],
            axis=1,
        )
        values = jnp.concatenate([values, jnp.zeros((LANES - owners, tile), F32)], axis=0)
        hi, low = split2(values)
        return mm(jnp.concatenate([pick, pick], axis=1), jnp.concatenate([hi, low], axis=0))

    def summed(terms):
        hi, low = split2(terms)
        return mm(scatter2, jnp.concatenate([hi, low], axis=0))

    def seen(half, lo):
        values = []
        for block in blocks:
            left = half * bins + lo if block.shape[1] == 2 * bins else half * total + lo - begin
            values.append(block[:, left : left + tile])
        return jnp.concatenate(values, axis=0)

    misfit = jnp.zeros((slots, tile), F32)
    for number, (first, last) in enumerate(spans):
        width = last - first
        mine = outs[sum(pieces[:number]) : sum(pieces[: number + 1])]

        def put(left, value):
            if starts:
                value = value + begun[number][:, left : left + tile]
            size = rows // len(mine)
            for piece, ref in enumerate(mine):
                ref[:, left : left + tile] = value[piece * size : (piece + 1) * size]

        for at in range(0, width, tile):
            lo = first + at
            index = lo + lax.broadcasted_iota(jnp.int32, (1, tile), 1)
            weights = 0.5 - 0.5 * jnp.cos((index.astype(F32) + 0.5) * (2.0 * math.pi / bins))
            receiver_real, receiver_imag = rows_of(lo), rows_of(bins + lo)
            source_real, source_imag = sources_of(lo), sources_of(bins + lo)
            diff_real = source_real * receiver_real + source_imag * receiver_imag - seen(0, lo)
            diff_imag = source_real * receiver_imag - source_imag * receiver_real - seen(1, lo)
            residual_real = weights * diff_real
            residual_imag = weights * diff_imag
            misfit = misfit + (residual_real * diff_real + residual_imag * diff_imag)
            put(at, summed(residual_real * source_real - residual_imag * source_imag))
            put(width + at, summed(residual_real * source_imag + residual_imag * source_real))
    misfit = jnp.sum(misfit, axis=1, keepdims=True) / (2 * bins)
    index = lax.broadcasted_iota(jnp.int32, (slots, capacity), 0) % capacity
    spots = lax.broadcasted_iota(jnp.int32, (slots, capacity), 1)
    spread = jnp.where(index == spots, misfit, 0.0)
    found = [
        jnp.sum(spread[number * capacity : (number + 1) * capacity], axis=0, keepdims=True)
        for number in range(len(tags))
    ]
    (misfit_ref,) = misfits
    if not last_of:
        for number in range(len(tags)):
            misfit_ref[number : number + 1, :] = found[number]
        return
    for ref, names in zip(before, older):
        for number, tag in enumerate(names):
            value = ref[number : number + 1, :]
            if tag in tags:
                found[tags.index(tag)] = found[tags.index(tag)] + value
            else:
                misfit_ref[pl.ds(here ^ tag, 1), :] = value
    for number, tag in enumerate(tags):
        misfit_ref[pl.ds(tag if whole_block else here ^ tag, 1), :] = found[number]


def look_kernel(returned_ref, slot_ref, out_ref):
    groups, capacity = returned_ref.shape
    slot = slot_ref[...]
    pairs = slot.shape[1]
    group = (
        lax.broadcasted_iota(jnp.int32, (groups, pairs), 0) == slot // capacity
    ).astype(F32).astype(BF16)
    parts = split3(returned_ref[...].T)
    values = mm(parts[0], group) + mm(parts[1], group) + mm(parts[2], group)
    rank = lax.broadcasted_iota(jnp.int32, (capacity, pairs), 0) == slot % capacity
    out_ref[...] = jnp.sum(jnp.where(rank, values, 0.0), axis=0, keepdims=True)


def inverse_kernel(
    scale, sizes, mix_ref, turn_cos_ref, turn_sin_ref, last_ref, *refs
):
    chunks = refs[: sum(sizes)]
    out_ref, held, wide = refs[-3:]
    count = out_ref.shape[0]
    blocks = held.shape[1] // 2
    turns = turn_cos_ref.shape[1]
    at = 0
    for number, size in enumerate(sizes):
        addends = chunks[sum(sizes[:number]) : sum(sizes[: number + 1])]
        width = addends[0].shape[1] // 2
        for block in range(width // LANES):
            for half in range(2):
                left = half * width + block * LANES
                value = addends[0][:count, left : left + LANES]
                for other in addends[1:]:
                    value = value + other[:count, left : left + LANES]
                held[:, half * blocks + at, :] = value
            at += 1
    mix = mix_ref[...]
    last = last_ref[...]
    turn_cos = turn_cos_ref[...]
    turn_sin = turn_sin_ref[...]
    for row in range(0, count, TOGETHER):
        some = range(row, row + TOGETHER)
        hi, low = split2(jnp.concatenate([held[i].T for i in some], axis=0))
        mixed = mm(jnp.concatenate([hi, low, hi], axis=1), mix)
        his, lows = [], []
        for i in range(TOGETHER):
            real = mixed[i * LANES : (i + 1) * LANES, :turns]
            imag = mixed[i * LANES : (i + 1) * LANES, turns:]
            hi, low = split2(
                jnp.concatenate(
                    [real * turn_cos - imag * turn_sin, real * turn_sin + imag * turn_cos], axis=0
                )
            )
            his.append(hi)
            lows.append(low)
        hi, low = jnp.concatenate(his, axis=1), jnp.concatenate(lows, axis=1)
        values = mm(last, jnp.concatenate([hi, low, hi], axis=0))
        for i, at in enumerate(some):
            wide[at] = values[:, i * turns : (i + 1) * turns]
    for block in range(wide.shape[1]):
        out_ref[:, block * LANES : (block + 1) * LANES] = wide[:, block, :] * scale


def bf16_parts(values):
    hi = values.astype(jnp.bfloat16)
    return hi, (values - hi.astype(np.float64)).astype(jnp.bfloat16)


def inverse(spectra, count, time_len, bins):
    period = 2 * time_len
    blocks = bins // LANES
    steps = period // LANES
    turns = LANES
    outer = time_len // turns
    cos, sin = phases(np.arange(steps)[:, None] * np.arange(blocks)[None, :] * LANES, period)
    mix = np.concatenate(
        [np.concatenate([cos, -sin], axis=1)] * (turns // steps)
        + [np.concatenate([sin, cos], axis=1)] * (turns // steps),
        axis=0,
    ).T
    hi, low = bf16_parts(mix)
    mix = np.concatenate([hi, hi, low], axis=0)
    r = np.arange(LANES)
    turn_cos, turn_sin = phases((K0 + r)[:, None] * np.arange(turns)[None, :], period)
    cos, sin = phases((K0 + r)[None, :] * np.arange(outer)[:, None] * turns, period)
    hi, low = bf16_parts(np.concatenate([cos, -sin], axis=1))
    last = np.concatenate([hi, hi, low], axis=1)
    chunks = [value for addends in spectra for value in addends]
    sizes = [len(addends) for addends in spectra]
    return pl.pallas_call(
        functools.partial(inverse_kernel, 1.0 / math.sqrt(bins), sizes),
        out_shape=jax.ShapeDtypeStruct((count, time_len), F32),
        in_specs=[VMEM] * (4 + len(chunks)),
        out_specs=VMEM,
        scratch_shapes=[
            pltpu.VMEM((count, 2 * blocks, LANES), F32),
            pltpu.VMEM((count, outer, LANES), F32),
        ],
        compiler_params=GRANT,
        cost_estimate=pl.CostEstimate(flops=1_000_000_000, bytes_accessed=2_000_000, transcendentals=0),
        name="inverse",
    )(
        in_hbm(mix), in_hbm(np.float32(turn_cos)), in_hbm(np.float32(turn_sin)), in_hbm(last),
        *chunks,
    )


def in_hbm(value):
    return pltpu.with_memory_space_constraint(jnp.asarray(value), pltpu.HBM)


def exchange(value, axis):
    return lax.all_to_all(value, axis, split_axis=0, concat_axis=0, tiled=True)


def over_src(value, step):
    return lax.ppermute(value, "src", [(i, i ^ step) for i in range(4)])


def rows_in_two(kept, sent):
    half = kept.shape[0] // 2
    moved = over_src(sent, 1)
    return [kept, moved, over_src(kept[half:] + moved[half:], 2)]


def rows_in_one(own, *others):
    return [own] + [over_src(value, step) for value, step in zip(others, (2, 1, 3))]


def per_device(records, virtual_sources, pair_group, pair_receiver, pair_source, observed):
    row_count, time_len = records.shape
    pair_count = observed.shape[0]
    bins = observed.shape[1] // 2
    groups = lax.axis_size("chan")
    assert lax.axis_size("src") == 4
    capacity = 2 * pair_count // groups
    slots = groups * capacity
    owners = virtual_sources.shape[0]
    chan_index = lax.axis_index("chan")
    routed = groups == 8
    part = 2 * bins // groups
    cut = bins * CUT // 8
    spans = [(0, cut), (cut, bins)]
    full = (0, bins)
    here = jnp.stack([chan_index if routed else 0 * chan_index, lax.axis_index("src")]).reshape(1, 2)
    smem = pl.BlockSpec(memory_space=pltpu.SMEM)
    lists = (
        here,
        in_hbm(pair_group.reshape(1, pair_count)),
        in_hbm(pair_receiver.reshape(1, pair_count)),
        in_hbm(pair_source.reshape(1, pair_count)),
    )

    def pack(parts, labelled):
        shapes = [
            jax.ShapeDtypeStruct(((high - low) * capacity, 2 * (last - first)), F32)
            for (low, high), (first, last) in parts
        ]
        if labelled:
            shapes.append(jax.ShapeDtypeStruct((groups, 8, part), F32))
            shapes.append(jax.ShapeDtypeStruct((1, pair_count), jnp.int32))
        return pl.pallas_call(
            functools.partial(pack_kernel, parts, groups),
            out_shape=shapes,
            in_specs=[smem] + [VMEM] * 4,
            out_specs=[VMEM] * len(shapes),
            compiler_params=GRANT,
            cost_estimate=pl.CostEstimate(flops=400_000_000, bytes_accessed=3_000_000, transcendentals=0),
            name="pack",
        )(*lists, observed)

    def move(value, tag):
        return lax.ppermute(value, "chan", [(i, i ^ tag) for i in range(groups)])

    if routed:
        *sent, label, slot = pack([((tag, tag + 1), full) for tag in FIRST], True)
        blocks = {tag: move(value, tag) for tag, value in zip(FIRST, sent)}
        rest = [*SECOND, *THIRD, *LATE]
        *sent, last_a, last_b, blocks[0] = pack(
            [((tag, tag + 1), full) for tag in rest]
            + [((LAST, LAST + 1), span) for span in spans]
            + [((0, 1), full)],
            False,
        )
    else:
        own, label, slot = pack([((0, groups), full)], True)

    period = 2 * time_len
    k = K0 + np.arange(bins)[None, :]
    cos_a, sin_a = phases(k * BASE * np.arange(time_len // BASE)[:, None], period)
    cos_b, sin_b = phases(k * np.arange(BASE)[:, None], period)
    steps = 4
    tile = bins // steps
    whole = lambda *shape: pl.BlockSpec(shape, lambda i: (0,) * len(shape))
    whitened, picked = pl.pallas_call(
        functools.partial(forward_kernel, steps),
        grid=(steps,),
        out_shape=[
            jax.ShapeDtypeStruct((row_count, 2 * bins), F32),
            jax.ShapeDtypeStruct((groups, owners + 8, part), F32),
        ],
        in_specs=[
            whole(row_count, time_len),
            *[pl.BlockSpec((value.shape[0], tile), lambda i: (0, i)) for value in (cos_a, cos_a, cos_b, cos_b)],
            whole(owners, 1), whole(groups, 8, part),
        ],
        out_specs=[whole(row_count, 2 * bins), whole(groups, owners + 8, part)],
        scratch_shapes=[pltpu.VMEM((time_len, tile), BF16)] * 2 + [pltpu.VMEM((row_count, 2 * bins), F32)],
        compiler_params=GRANT,
        cost_estimate=pl.CostEstimate(flops=8_000_000_000, bytes_accessed=4_000_000, transcendentals=0),
        name="forward",
    )(
        records, in_hbm(np.float32(cos_a)), in_hbm(np.float32(-sin_a)), in_hbm(np.float32(cos_b)),
        in_hbm(np.float32(-sin_b)), (virtual_sources - chan_index * row_count).reshape(owners, 1), label,
    )

    arrived = exchange(picked, "chan")
    summed = pl.pallas_call(
        spread_kernel,
        out_shape=jax.ShapeDtypeStruct((groups, owners, part), F32),
        in_specs=[VMEM],
        out_specs=VMEM,
        compiler_params=GRANT,
        cost_estimate=pl.CostEstimate(flops=100_000, bytes_accessed=300_000, transcendentals=0),
        name="spread",
    )(arrived)
    sources = exchange(summed, "chan")

    def terms(values, tags, some, split, begun, before, older=(), last_of=False):
        shapes = [
            jax.ShapeDtypeStruct((row_count // pieces, 2 * (last - first)), F32)
            for (first, last), pieces in zip(some, split)
            for _ in range(pieces)
        ] + [jax.ShapeDtypeStruct((groups if last_of else len(tags), capacity), F32)]
        return pl.pallas_call(
            functools.partial(
                pair_kernel, bins, some, tags, not routed, len(begun), older, last_of, split
            ),
            out_shape=shapes,
            in_specs=[smem] + [VMEM] * (3 + len(values) + len(begun) + len(before)),
            out_specs=[VMEM] * len(shapes),
            compiler_params=GRANT,
            cost_estimate=pl.CostEstimate(flops=2_000_000_000, bytes_accessed=5_000_000, transcendentals=0),
            name="pairs",
        )(here, arrived, whitened, sources, *values, *begun, *before)

    if routed:
        for tag, value in zip(rest, sent):
            blocks[tag] = move(value, tag)
        last_a = move(last_a, LAST)
        last_b = move(last_b, LAST)
        *begun, misfit = terms([blocks[tag] for tag in EARLY], EARLY, spans, (1, 1), [], [])
        older, before = [EARLY], [misfit]
        tags = [*LATE, LAST]
        late = [blocks[tag] for tag in LATE]
        *sums, misfit = terms([*late, last_a], tags, spans[:1], (2,), begun[:1], [])
        older.append(tags)
        before.append(misfit)
        spectra = [rows_in_two(*sums)]
        *sums, misfit = terms([*late, last_b], tags, spans[1:], (4,), begun[1:], before, older, True)
        spectra.append(rows_in_one(*sums))
    else:
        came = exchange(own.reshape(groups, capacity, -1), "chan").reshape(slots, -1)
        *sums, misfit = terms([came], list(range(groups)), spans, (2, 2), [], [], (), True)
        spectra = [rows_in_two(*sums[:2]), rows_in_two(*sums[2:])]

    returned = exchange(misfit, "chan")
    result = inverse(spectra, row_count // 4, time_len, bins)
    pair_misfit = pl.pallas_call(
        look_kernel,
        out_shape=jax.ShapeDtypeStruct((1, pair_count), F32),
        in_specs=[VMEM] * 2,
        out_specs=VMEM,
        compiler_params=GRANT,
        cost_estimate=pl.CostEstimate(flops=100_000, bytes_accessed=3000, transcendentals=0),
        name="look",
    )(returned, slot)
    return (result, pair_misfit.reshape(pair_count))


def solution(mesh):
    return jax.shard_map(
        per_device,
        mesh=mesh,
        in_specs=(
            P("chan", None),
            P("src"),
            P(("chan", "src"), None),
            P(("chan", "src")),
            P(("chan", "src")),
            P(("chan", "src"), None),
        ),
        out_specs=(P(("chan", "src"), None), P(("chan", "src"))),
        check_vma=False,
    )
```

```python
import functools
import math

import jax
import jax.numpy as jnp
import numpy as np
from jax import lax
from jax.experimental import pallas as pl
from jax.experimental.pallas import tpu as pltpu
from jax.sharding import PartitionSpec as P


K0 = 64
LANES = 128
CUT = 4
TOGETHER = 4
GRANT = pltpu.CompilerParams(vmem_limit_bytes=12 * 1024 * 1024)
FIRST = (5,)
SECOND = (6,)
THIRD = (2, 3, 1)
LATE = (7,)
LAST = 4
EARLY = [0, *FIRST, *SECOND, *THIRD]
BASE = 64
F32 = jnp.float32
BF16 = jnp.bfloat16
VMEM = pl.BlockSpec(memory_space=pltpu.VMEM)
NT_DIMS = (((1,), (1,)), ((), ()))


def mm(a, b):
    return jnp.dot(a, b, preferred_element_type=F32)


def split2(x):
    hi = x.astype(BF16)
    return hi, (x - hi.astype(F32)).astype(BF16)


def split3(x):
    hi = x.astype(BF16)
    rest = x - hi.astype(F32)
    mid = rest.astype(BF16)
    return hi, mid, (rest - mid.astype(F32)).astype(BF16)


def phases(products, period):
    angles = (products % period) * (2.0 * math.pi / period)
    return np.cos(angles), np.sin(angles)


def pack_kernel(parts, groups, here_ref, group_ref, receiver_ref, source_ref, observed_ref, *outs):
    pairs = observed_ref.shape[0]
    bins = observed_ref.shape[1] // 2
    capacity = 2 * pairs // groups
    group_row = group_ref[...]
    hits = (
        lax.broadcasted_iota(jnp.int32, (max(groups, 8), pairs), 0) == group_row
    ).astype(F32)
    earlier = (
        lax.broadcasted_iota(jnp.int32, (pairs, pairs), 0)
        < lax.broadcasted_iota(jnp.int32, (pairs, pairs), 1)
    ).astype(F32)
    counts = mm(hits.astype(BF16), earlier.astype(BF16))
    rank = jnp.sum(hits * counts, axis=0, keepdims=True).astype(jnp.int32)

    def chosen(slot_row, start, stop):
        index = start + lax.broadcasted_iota(jnp.int32, (stop - start, pairs), 0)
        return (index == slot_row).astype(F32).astype(BF16)

    if len(outs) > len(parts):
        label_ref, slot_ref = outs[-2:]
        slot_row = group_row * capacity + rank
        slot_ref[...] = slot_row
        labels = jnp.concatenate(
            [receiver_ref[...] + 1, source_ref[...]] + [jnp.zeros((6, pairs), jnp.int32)], axis=0
        ).astype(F32).astype(BF16)
        sent = lax.dot_general(
            labels, chosen(slot_row, 0, groups * capacity), NT_DIMS, preferred_element_type=F32
        )
        code = jnp.broadcast_to(sent[0:1] * 256.0 + sent[1:2], (8, groups * capacity))
        label_ref[...] = jnp.zeros_like(label_ref)
        for group in range(groups):
            label_ref[group, :, :capacity] = code[:, group * capacity : (group + 1) * capacity]
    slot_row = (group_row ^ here_ref[0, 0]) * capacity + rank
    for span in dict.fromkeys(part[1] for part in parts):
        mine = [(tags, ref) for (tags, other), ref in zip(parts, outs) if other == span]
        rows = jnp.concatenate(
            [chosen(slot_row, low * capacity, high * capacity) for (low, high), _ in mine], axis=0
        )
        rows = jnp.concatenate([rows] * 3, axis=1)
        width = span[1] - span[0]
        tile = math.gcd(width, 256)
        for half in range(2):
            for at in range(0, width, tile):
                left = half * bins + span[0] + at
                values = mm(rows, jnp.concatenate(split3(observed_ref[:, left : left + tile]), axis=0))
                top = 0
                for (low, high), out_ref in mine:
                    count = (high - low) * capacity
                    out_ref[:, half * width + at : half * width + at + tile] = values[top : top + count]
                    top += count


def forward_kernel(
    steps, records_ref, cos_a_ref, sin_a_ref, cos_b_ref, sin_b_ref, rows_ref, label_ref,
    white_ref, picked_ref, table_real, table_imag, total,
):
    step = pl.program_id(0)
    width = cos_b_ref.shape[1]
    bins = steps * width
    cos_b, sin_b = cos_b_ref[...], sin_b_ref[...]
    for row in range(cos_a_ref.shape[0]):
        cos_a, sin_a = cos_a_ref[row : row + 1, :], sin_a_ref[row : row + 1, :]
        rows = slice(row * BASE, (row + 1) * BASE)
        table_real[rows, :] = (cos_a * cos_b - sin_a * sin_b).astype(BF16)
        table_imag[rows, :] = (sin_a * cos_b + cos_a * sin_b).astype(BF16)
    left = pl.multiple_of(step * width, width)
    total[:, pl.ds(left, width)] = mm(records_ref[...], table_real[...])
    total[:, pl.ds(bins + left, width)] = mm(records_ref[...], table_imag[...])

    @pl.when(step == steps - 1)
    def _():
        spectra = total[...]
        power = jnp.sum(spectra * spectra, axis=1, keepdims=True) / bins
        white = spectra / jnp.sqrt(power + 1e-06)
        white_ref[...] = white
        owners = rows_ref.shape[0]
        chosen = (
            lax.broadcasted_iota(jnp.int32, (owners, white.shape[0]), 1) == rows_ref[...]
        ).astype(F32).astype(BF16)
        picked = mm(jnp.concatenate([chosen] * 3, axis=1), jnp.concatenate(split3(white), axis=0))
        part = picked_ref.shape[2]
        for group in range(picked_ref.shape[0]):
            picked_ref[group, :owners, :] = picked[:, group * part : (group + 1) * part]
        picked_ref[:, owners:, :] = label_ref[...]


def stage_kernel(*refs):
    for source, target in zip(refs[: len(refs) // 2], refs[len(refs) // 2 :]):
        target[...] = source[...]


def spread_kernel(arrived_ref, out_ref):
    owners = out_ref.shape[1]
    summed = arrived_ref[0, :owners, :]
    for group in range(1, arrived_ref.shape[0]):
        summed = summed + arrived_ref[group, :owners, :]
    out_ref[...] = jnp.broadcast_to(summed[None], out_ref.shape)


def pair_kernel(
    bins, spans, tags, whole_block, starts, older, last_of, split, here_ref, arrived_ref, white_ref, sources_ref, *refs
):
    count = 1 if whole_block else len(tags)
    pieces = split
    refs = list(refs)
    blocks, begun = refs[:count], refs[count : count + starts]
    before = refs[count + starts : count + starts + len(older)]
    refs = refs[count + starts + len(older) :]
    outs, misfits = refs[: sum(pieces)], refs[sum(pieces) :]
    begin = spans[0][0]
    total = spans[-1][1] - begin
    rows = white_ref.shape[0]
    _, owners, part = sources_ref.shape
    capacity = misfits[0].shape[1]
    here, side = here_ref[0, 0], here_ref[0, 1]
    quarter = rows // 4
    gathers, picks = [], []
    for tag in tags:
        code = arrived_ref[tag if whole_block else here ^ tag, owners : owners + 8, :capacity]
        code = code[0:1, :].astype(jnp.int32)
        receiver = code // 256 - 1
        source = code % 256
        hit = (lax.broadcasted_iota(jnp.int32, (rows, capacity), 0) == receiver).astype(F32)
        gathers.append(hit.T)
        hit = (
            (lax.broadcasted_iota(jnp.int32, (LANES, capacity), 0) == source) & (receiver >= 0)
        ).astype(F32)
        picks.append(hit.T)
    gather = jnp.concatenate(gathers, axis=0)
    pick = jnp.concatenate(picks, axis=0).astype(BF16)
    place = lax.broadcasted_iota(jnp.int32, (rows, rows), 0)
    block = place // quarter
    block = (((block & 1) << 1) | (block >> 1)) ^ side
    wanted = block * quarter + place % quarter
    order = (lax.broadcasted_iota(jnp.int32, (rows, rows), 1) == wanted).astype(F32).astype(BF16)
    gather2 = gather.astype(BF16)
    scatter = lax.dot_general(order, gather2, NT_DIMS, preferred_element_type=F32).astype(BF16)
    gather2 = jnp.concatenate([gather2, gather2], axis=1)
    scatter2 = jnp.concatenate([scatter, scatter], axis=1)
    slots = gather.shape[0]

    def rows_of(left, tile):
        hi, low = split2(white_ref[:, left : left + tile])
        return mm(gather2, jnp.concatenate([hi, low], axis=0))

    def sources_of(left, tile):
        taken = min(LANES, part)
        values = jnp.concatenate(
            [sources_ref[at // part, :, at % part : at % part + taken] for at in range(left, left + tile, taken)],
            axis=1,
        )
        values = jnp.concatenate([values, jnp.zeros((LANES - owners, tile), F32)], axis=0)
        hi, low = split2(values)
        return mm(jnp.concatenate([pick, pick], axis=1), jnp.concatenate([hi, low], axis=0))

    def summed(terms):
        hi, low = split2(terms)
        return mm(scatter2, jnp.concatenate([hi, low], axis=0))

    def seen(half, lo, tile):
        values = []
        for block in blocks:
            left = half * bins + lo if block.shape[1] == 2 * bins else half * total + lo - begin
            values.append(block[:, left : left + tile])
        return jnp.concatenate(values, axis=0)

    misfit = jnp.zeros((slots, LANES), F32)
    for number, (first, last) in enumerate(spans):
        width = last - first
        mine = outs[sum(pieces[:number]) : sum(pieces[: number + 1])]

        def put(left, tile, value):
            if starts:
                value = value + begun[number][:, left : left + tile]
            size = rows // len(mine)
            for piece, ref in enumerate(mine):
                ref[:, left : left + tile] = value[piece * size : (piece + 1) * size]

        for at in range(0, width, 2 * LANES):
            tile = min(2 * LANES, width - at)
            lo = first + at
            index = lo + lax.broadcasted_iota(jnp.int32, (1, tile), 1)
            weights = 0.5 - 0.5 * jnp.cos((index.astype(F32) + 0.5) * (2.0 * math.pi / bins))
            receiver_real, receiver_imag = rows_of(lo, tile), rows_of(bins + lo, tile)
            source_real, source_imag = sources_of(lo, tile), sources_of(bins + lo, tile)
            diff_real = source_real * receiver_real + source_imag * receiver_imag - seen(0, lo, tile)
            diff_imag = source_real * receiver_imag - source_imag * receiver_real - seen(1, lo, tile)
            residual_real = weights * diff_real
            residual_imag = weights * diff_imag
            weighted = residual_real * diff_real + residual_imag * diff_imag
            for lane in range(0, tile, LANES):
                misfit = misfit + weighted[:, lane : lane + LANES]
            put(at, tile, summed(residual_real * source_real - residual_imag * source_imag))
            put(width + at, tile, summed(residual_real * source_imag + residual_imag * source_real))
    misfit = jnp.sum(misfit, axis=1, keepdims=True) / (2 * bins)
    index = lax.broadcasted_iota(jnp.int32, (slots, capacity), 0) % capacity
    spots = lax.broadcasted_iota(jnp.int32, (slots, capacity), 1)
    spread = jnp.where(index == spots, misfit, 0.0)
    found = [
        jnp.sum(spread[number * capacity : (number + 1) * capacity], axis=0, keepdims=True)
        for number in range(len(tags))
    ]
    (misfit_ref,) = misfits
    if not last_of:
        for number in range(len(tags)):
            misfit_ref[number : number + 1, :] = found[number]
        return
    for ref, names in zip(before, older):
        for number, tag in enumerate(names):
            value = ref[number : number + 1, :]
            if tag in tags:
                found[tags.index(tag)] = found[tags.index(tag)] + value
            else:
                misfit_ref[pl.ds(here ^ tag, 1), :] = value
    for number, tag in enumerate(tags):
        misfit_ref[pl.ds(tag if whole_block else here ^ tag, 1), :] = found[number]


def look_kernel(returned_ref, slot_ref, out_ref):
    groups, capacity = returned_ref.shape
    slot = slot_ref[...]
    pairs = slot.shape[1]
    group = (
        lax.broadcasted_iota(jnp.int32, (groups, pairs), 0) == slot // capacity
    ).astype(F32).astype(BF16)
    parts = split3(returned_ref[...].T)
    values = mm(parts[0], group) + mm(parts[1], group) + mm(parts[2], group)
    rank = lax.broadcasted_iota(jnp.int32, (capacity, pairs), 0) == slot % capacity
    out_ref[...] = jnp.sum(jnp.where(rank, values, 0.0), axis=0, keepdims=True)


def inverse_kernel(
    scale, sizes, mix_ref, turn_cos_ref, turn_sin_ref, last_ref, *refs
):
    chunks = refs[: sum(sizes)]
    out_ref, held, wide = refs[-3:]
    count = out_ref.shape[0]
    blocks = held.shape[1] // 2
    at = 0
    for number, size in enumerate(sizes):
        addends = chunks[sum(sizes[:number]) : sum(sizes[: number + 1])]
        width = addends[0].shape[1] // 2
        for block in range(width // LANES):
            for half in range(2):
                left = half * width + block * LANES
                value = addends[0][:count, left : left + LANES]
                for other in addends[1:]:
                    value = value + other[:count, left : left + LANES]
                held[:, half * blocks + at, :] = value
            at += 1
    mix = mix_ref[...]
    last = last_ref[...]
    turn_cos = turn_cos_ref[...]
    turn_sin = turn_sin_ref[...]
    outer = last.shape[0] // 2
    first_row = lax.broadcasted_iota(jnp.int32, (outer, LANES), 1) < LANES // 2
    for row in range(0, count, TOGETHER):
        sides = []
        for pair in range(row, row + TOGETHER, 2):
            parts = []
            for i in (pair, pair + 1):
                hi, low = split2(held[i].T)
                parts += [hi, low, hi]
            sides.append(jnp.concatenate(parts, axis=1))
        mixed = mm(jnp.concatenate(sides, axis=0), mix)
        his, lows = [], []
        for i in range(TOGETHER // 2):
            real = mixed[i * LANES : (i + 1) * LANES, :LANES]
            imag = mixed[i * LANES : (i + 1) * LANES, LANES:]
            hi, low = split2(
                jnp.concatenate(
                    [real * turn_cos - imag * turn_sin, real * turn_sin + imag * turn_cos], axis=0
                )
            )
            his.append(hi)
            lows.append(low)
        hi, low = jnp.concatenate(his, axis=1), jnp.concatenate(lows, axis=1)
        values = mm(last, jnp.concatenate([hi, low, hi], axis=0))
        for i in range(TOGETHER // 2):
            even = values[:outer, i * LANES : (i + 1) * LANES]
            odd = values[outer:, i * LANES : (i + 1) * LANES]
            at = row + 2 * i
            wide[at] = jnp.where(first_row, even, pltpu.roll(odd, LANES // 2, 1))
            wide[at + 1] = jnp.where(first_row, pltpu.roll(even, LANES // 2, 1), odd)
    for block in range(wide.shape[1]):
        out_ref[:, block * LANES : (block + 1) * LANES] = wide[:, block, :] * scale


def bf16_parts(values):
    hi = values.astype(jnp.bfloat16)
    return hi, (values - hi.astype(np.float64)).astype(jnp.bfloat16)


def inverse_tables(time_len, bins):
    period = 2 * time_len
    blocks = bins // LANES
    steps = period // LANES
    assert 2 * steps == LANES
    outer = time_len // steps
    b, r = np.arange(steps), np.arange(LANES)
    cos, sin = phases(b[None, :] * np.arange(blocks)[:, None] * LANES, period)
    columns = []
    for part in (np.concatenate([cos, -sin]), np.concatenate([sin, cos])):
        hi, low = bf16_parts(part)
        columns.append(np.concatenate([hi, hi, low]))
    real, imag = columns
    none = np.zeros_like(real)
    mix = np.block([[real, none, imag, none], [none, real, none, imag]]).astype(real.dtype)
    turn_cos, turn_sin = phases((K0 + r)[:, None] * np.tile(b, 2)[None, :], period)
    a = np.concatenate([np.arange(0, outer, 2), np.arange(1, outer, 2)])
    cos, sin = phases((K0 + r)[None, :] * a[:, None] * steps, period)
    hi, low = bf16_parts(np.concatenate([cos, -sin], axis=1))
    last = np.concatenate([hi, hi, low], axis=1)
    return mix, np.float32(turn_cos), np.float32(turn_sin), last


def inverse(tables, spectra, count, time_len, bins):
    blocks = bins // LANES
    chunks = [value for addends in spectra for value in addends]
    sizes = [len(addends) for addends in spectra]
    return pl.pallas_call(
        functools.partial(inverse_kernel, 1.0 / math.sqrt(bins), sizes),
        out_shape=jax.ShapeDtypeStruct((count, time_len), F32),
        in_specs=[VMEM] * (4 + len(chunks)),
        out_specs=VMEM,
        scratch_shapes=[
            pltpu.VMEM((count, 2 * blocks, LANES), F32),
            pltpu.VMEM((count, time_len // LANES, LANES), F32),
        ],
        compiler_params=GRANT,
        cost_estimate=pl.CostEstimate(flops=1_000_000_000, bytes_accessed=2_000_000, transcendentals=0),
        name="inverse",
    )(
        *tables,
        *chunks,
    )


def in_hbm(value):
    return pltpu.with_memory_space_constraint(jnp.asarray(value), pltpu.HBM)


def exchange(value, axis):
    return lax.all_to_all(value, axis, split_axis=0, concat_axis=0, tiled=True)


def over_src(value, step):
    return lax.ppermute(value, "src", [(i, i ^ step) for i in range(4)])


def rows_in_two(kept, sent):
    half = kept.shape[0] // 2
    moved = over_src(sent, 1)
    return [kept, moved, over_src(kept[half:] + moved[half:], 2)]


def rows_in_one(own, *others):
    return [own] + [over_src(value, step) for value, step in zip(others, (2, 1, 3))]


def per_device(records, virtual_sources, pair_group, pair_receiver, pair_source, observed):
    row_count, time_len = records.shape
    pair_count = observed.shape[0]
    bins = observed.shape[1] // 2
    groups = lax.axis_size("chan")
    assert lax.axis_size("src") == 4
    capacity = 2 * pair_count // groups
    slots = groups * capacity
    owners = virtual_sources.shape[0]
    chan_index = lax.axis_index("chan")
    routed = groups == 8
    part = 2 * bins // groups
    cut = bins * CUT // 8
    spans = [(0, cut), (cut, bins)]
    full = (0, bins)
    here = jnp.stack([chan_index if routed else 0 * chan_index, lax.axis_index("src")]).reshape(1, 2)
    smem = pl.BlockSpec(memory_space=pltpu.SMEM)
    lists = (
        here,
        in_hbm(pair_group.reshape(1, pair_count)),
        in_hbm(pair_receiver.reshape(1, pair_count)),
        in_hbm(pair_source.reshape(1, pair_count)),
    )

    def pack(parts, labelled):
        shapes = [
            jax.ShapeDtypeStruct(((high - low) * capacity, 2 * (last - first)), F32)
            for (low, high), (first, last) in parts
        ]
        if labelled:
            shapes.append(jax.ShapeDtypeStruct((groups, 8, part), F32))
            shapes.append(jax.ShapeDtypeStruct((1, pair_count), jnp.int32))
        return pl.pallas_call(
            functools.partial(pack_kernel, parts, groups),
            out_shape=shapes,
            in_specs=[smem] + [VMEM] * 4,
            out_specs=[VMEM] * len(shapes),
            compiler_params=GRANT,
            cost_estimate=pl.CostEstimate(flops=400_000_000, bytes_accessed=3_000_000, transcendentals=0),
            name="pack",
        )(*lists, observed)

    def move(value, tag):
        return lax.ppermute(value, "chan", [(i, i ^ tag) for i in range(groups)])

    if routed:
        *sent, label, slot = pack([((tag, tag + 1), full) for tag in FIRST], True)
        blocks = {tag: move(value, tag) for tag, value in zip(FIRST, sent)}
        rest = [*SECOND, *THIRD, *LATE]
        *sent, last_a, last_b, blocks[0] = pack(
            [((tag, tag + 1), full) for tag in rest]
            + [((LAST, LAST + 1), span) for span in spans]
            + [((0, 1), full)],
            False,
        )
    else:
        own, label, slot = pack([((0, groups), full)], True)

    period = 2 * time_len
    k = K0 + np.arange(bins)[None, :]
    cos_a, sin_a = phases(k * BASE * np.arange(time_len // BASE)[:, None], period)
    cos_b, sin_b = phases(k * np.arange(BASE)[:, None], period)
    steps = 4
    tile = bins // steps
    whole = lambda *shape: pl.BlockSpec(shape, lambda i: (0,) * len(shape))
    whitened, picked = pl.pallas_call(
        functools.partial(forward_kernel, steps),
        grid=(steps,),
        out_shape=[
            pltpu.HBM((row_count, 2 * bins), F32),
            jax.ShapeDtypeStruct((groups, owners + 8, part), F32),
        ],
        in_specs=[
            whole(row_count, time_len),
            *[pl.BlockSpec((value.shape[0], tile), lambda i: (0, i)) for value in (cos_a, cos_a, cos_b, cos_b)],
            whole(owners, 1), whole(groups, 8, part),
        ],
        out_specs=[whole(row_count, 2 * bins), whole(groups, owners + 8, part)],
        scratch_shapes=[pltpu.VMEM((time_len, tile), BF16)] * 2 + [pltpu.VMEM((row_count, 2 * bins), F32)],
        compiler_params=GRANT,
        cost_estimate=pl.CostEstimate(flops=8_000_000_000, bytes_accessed=4_000_000, transcendentals=0),
        name="forward",
    )(
        records, in_hbm(np.float32(cos_a)), in_hbm(np.float32(-sin_a)), in_hbm(np.float32(cos_b)),
        in_hbm(np.float32(-sin_b)), (virtual_sources - chan_index * row_count).reshape(owners, 1), label,
    )

    arrived = exchange(picked, "chan")
    summed = pl.pallas_call(
        spread_kernel,
        out_shape=jax.ShapeDtypeStruct((groups, owners, part), F32),
        in_specs=[VMEM],
        out_specs=VMEM,
        compiler_params=GRANT,
        cost_estimate=pl.CostEstimate(flops=100_000, bytes_accessed=300_000, transcendentals=0),
        name="spread",
    )(arrived)
    sources = exchange(summed, "chan")

    def terms(values, tags, some, split, begun, before, older=(), last_of=False):
        shapes = [
            jax.ShapeDtypeStruct((row_count // pieces, 2 * (last - first)), F32)
            for (first, last), pieces in zip(some, split)
            for _ in range(pieces)
        ] + [jax.ShapeDtypeStruct((groups if last_of else len(tags), capacity), F32)]
        return pl.pallas_call(
            functools.partial(
                pair_kernel, bins, some, tags, not routed, len(begun), older, last_of, split
            ),
            out_shape=shapes,
            in_specs=[smem] + [VMEM] * (3 + len(values) + len(begun) + len(before)),
            out_specs=[VMEM] * len(shapes),
            compiler_params=GRANT,
            cost_estimate=pl.CostEstimate(flops=2_000_000_000, bytes_accessed=5_000_000, transcendentals=0),
            name="pairs",
        )(here, arrived, whitened, sources, *values, *begun, *before)

    tables = inverse_tables(time_len, bins)
    tables = pl.pallas_call(
        stage_kernel,
        out_shape=[jax.ShapeDtypeStruct(table.shape, table.dtype) for table in tables],
        in_specs=[VMEM] * 4,
        out_specs=[VMEM] * 4,
        compiler_params=GRANT,
        cost_estimate=pl.CostEstimate(flops=1000, bytes_accessed=1_000_000, transcendentals=0),
        name="stage",
    )(*[in_hbm(table) for table in tables])

    if routed:
        for tag, value in zip(rest, sent):
            blocks[tag] = move(value, tag)
        last_a = move(last_a, LAST)
        last_b = move(last_b, LAST)
        *begun, misfit = terms([blocks[tag] for tag in EARLY], EARLY, spans, (1, 1), [], [])
        older, before = [EARLY], [misfit]
        tags = [*LATE, LAST]
        late = [blocks[tag] for tag in LATE]
        *sums, misfit = terms([*late, last_a], tags, spans[:1], (2,), begun[:1], [])
        older.append(tags)
        before.append(misfit)
        spectra = [rows_in_two(*sums)]
        *sums, misfit = terms([*late, last_b], tags, spans[1:], (4,), begun[1:], before, older, True)
        spectra.append(rows_in_one(*sums))
    else:
        came = exchange(own.reshape(groups, capacity, -1), "chan").reshape(slots, -1)
        *sums, misfit = terms([came], list(range(groups)), spans, (2, 2), [], [], (), True)
        spectra = [rows_in_two(*sums[:2]), rows_in_two(*sums[2:])]

    returned = exchange(misfit, "chan")
    result = inverse(tables, spectra, row_count // 4, time_len, bins)
    pair_misfit = pl.pallas_call(
        look_kernel,
        out_shape=jax.ShapeDtypeStruct((1, pair_count), F32),
        in_specs=[VMEM] * 2,
        out_specs=VMEM,
        compiler_params=GRANT,
        cost_estimate=pl.CostEstimate(flops=100_000, bytes_accessed=3000, transcendentals=0),
        name="look",
    )(returned, slot)
    return (result, pair_misfit.reshape(pair_count))


def solution(mesh):
    return jax.shard_map(
        per_device,
        mesh=mesh,
        in_specs=(
            P("chan", None),
            P("src"),
            P(("chan", "src"), None),
            P(("chan", "src")),
            P(("chan", "src")),
            P(("chan", "src"), None),
        ),
        out_specs=(P(("chan", "src"), None), P(("chan", "src"))),
        check_vma=False,
    )
```
